32 devices in a mesh: groups: 2 (over y), ctx: 4 (over z), fsdp: 4 (over x, core).
Axes of the slice: x: 2, y: 2, z: 4, core: 2. Of those that a mesh axis runs over, the one named last changes fastest.
Arguments:
- patches: bfloat16 [8192, 1024], P(('groups', 'ctx', 'fsdp')), parts along dimension 0, may hold values from -6 to 6
- labels: int32 [8192], P(('groups', 'ctx', 'fsdp')), parts along dimension 0, may hold values from 0 to 127
- op_ids: int32 [4, 3], P('groups'), parts along dimension 0, may hold values from 0 to 8
- mix_codes: int32 [4, 4], P('groups'), parts along dimension 0, may hold values from 1 to 8
- aug_gains: float32 [9, 1024], replicated, may hold values from 0.1 to 1.9
- in_weight: bfloat16 [1024, 1536], P('fsdp'), may hold values from -0.1875 to 0.1875
- dt_weight: bfloat16 [1024, 32], P('fsdp'), may hold values from -0.09375 to 0.09375
- dt_bias: float32 [2, 16], replicated, may hold values from -3.9 to -2.2
- decay_log: float32 [2, 16], replicated, may hold values from -12 to 0
- skip_gain: float32 [16], replicated, may hold values from 0.1 to 1.9
- norm_gain: float32 [1024], replicated, may hold values from 0.5 to 1.5
- out_weight: bfloat16 [1024, 1024], P('fsdp'), may hold values from -0.1875 to 0.1875
- head_weight: bfloat16 [1024, 128], replicated, may hold values from -8 to 8
Outputs:
- grad_out: float32 [2048, 1024], P(('groups', 'ctx', 'fsdp')), parts along dimension 0
- grad_head: float32 [2048, 128], P(('groups', 'ctx', 'fsdp')), parts along dimension 0
- patch_loss: float32 [8192], P(('groups', 'ctx', 'fsdp')), parts along dimension 0
The draws below stay inside these ranges and needn't reach their ends.
There are 2 independent parts, one for each index of `groups`. The reference program is written for one: setup_inputs(seed, part) draws one part's arguments, and reference() takes and returns one part's arrays. A program takes and returns all parts, laid end to end along the dimension named above; an argument that names none is the same for every part. Nothing has to cross between parts.
All inputs are finite; a program needn't handle non-finite values.
Results may differ from the reference program's by a relative error of at most 0.01505.
The reference program's roundings to bfloat16 on the way (of `views`, `projected`, `normed`, `hidden`, `grad_logits` and `grad_hidden`) count: a program that leaves them out, or rounds other values in their place, can miss the bound.
Values may be sent and summed in bfloat16 or wider, within the bound.
A program may use at most 128 MiB of HBM per device.

```python
import math
import jax
import jax.numpy as jnp
from jax import lax

D = 1024
HEADS = 16
HEAD_DIM = 64
STATE = 128
CLASSES = 128
VIEWS = 3
NOPS = 9
WIDTH_AUG = 3
BLOCK = 128
DIN = 1024
PROJ = 1536
PATCHES = 4096


def draw_decay_log(key, part):
    pick_key = jax.random.fold_in(key, 11)
    slow_key = jax.random.fold_in(key, 12)
    fast_key = jax.random.fold_in(key, 13)
    slow_share = 0.5
    slow_pick = jax.random.uniform(pick_key, (2, HEADS), jnp.float32) < slow_share
    slow_rate = jax.random.uniform(slow_key, (2, HEADS), jnp.float32, minval=math.log(4.0 / PATCHES), maxval=math.log(40.0 / PATCHES))
    fast_rate = jax.random.uniform(fast_key, (2, HEADS), jnp.float32, minval=math.log(0.4), maxval=0.0)
    return jnp.where(slow_pick, slow_rate, fast_rate).astype(jnp.float32)


def draw_head_weight(key, part):
    spread_factor = 3.0
    drawn = jax.random.normal(jax.random.fold_in(key, 21), (D, CLASSES), jnp.float32) * (spread_factor / math.sqrt(D))
    return jnp.clip(drawn, -8.0, 8.0).astype(jnp.bfloat16)


def plant(values, key, low, top_value):
    place = [jax.random.randint(jax.random.fold_in(key, axis), (), 0, length) for axis, length in enumerate(values.shape)]
    longest = values.shape.index(max(values.shape))
    beside = place[:longest] + [(place[longest] + 1) % values.shape[longest]] + place[longest + 1:]
    return values.at[tuple(place)].set(low).at[tuple(beside)].set(top_value)


def steps_of(stream_key, extent, cuts, low, top_value):
    loudness = 1.0
    for axis_at, shards_of in cuts:
        steps = jax.random.uniform(jax.random.fold_in(jax.random.fold_in(stream_key, 6), axis_at), (shards_of,), jnp.float32, low / len(cuts), top_value / len(cuts))
        loudness = loudness * jnp.repeat(jnp.exp(steps), extent[axis_at] // shards_of).reshape((-1,) + (1,) * (len(extent) - 1 - axis_at))
    return loudness


def normal_values(own_key, dims, width, bound, split=(), kind=jnp.bfloat16):
    level = steps_of(own_key, dims, split, -0.22, 0.18) if split else 1.0
    values = jax.random.normal(own_key, dims, jnp.float32) * width * level
    return jnp.minimum(jnp.maximum(values, -bound), bound).astype(kind)


def setup_inputs(seed: int = 0, part: int = 0) -> dict:
    seeds = jax.random.split(jax.random.key(seed), 14)
    part_keys = jax.random.split(jax.random.fold_in(seeds[13], part), 14)
    patches = normal_values(part_keys[0], (PATCHES, D), 1.0, 6.0, ((0, 16),))
    labels = plant(jax.random.randint(part_keys[1], (PATCHES,), 0, CLASSES), jax.random.fold_in(part_keys[1], 1), 0, CLASSES - 1).astype(jnp.int32)
    op_ids = plant(jax.random.randint(part_keys[2], (2, WIDTH_AUG), 0, NOPS), jax.random.fold_in(part_keys[2], 1), 0, NOPS - 1).astype(jnp.int32)
    mix_codes = plant(jax.random.randint(part_keys[3], (2, WIDTH_AUG + 1), 1, 9), jax.random.fold_in(part_keys[3], 1), 1, 8).astype(jnp.int32)
    aug_gains = jnp.clip(1.0 + 0.18 * jax.random.normal(seeds[4], (NOPS, D), jnp.float32), 0.1, 1.9)
    in_weight = normal_values(seeds[5], (D, PROJ), D ** -0.5, 0.1875, ((0, 4),))
    dt_weight = normal_values(seeds[6], (D, 2 * HEADS), (4 * D) ** -0.5, 0.09375, ((0, 4),))
    dt_bias = jnp.clip(jax.random.uniform(seeds[7], (2, HEADS), jnp.float32, -3.9, -2.2), -3.9, -2.2)
    decay_log = draw_decay_log(jax.random.fold_in(seeds[13], 71), part)
    skip_gain = jnp.clip(1.0 + 0.18 * jax.random.normal(seeds[9], (HEADS,), jnp.float32), 0.1, 1.9)
    norm_gain = jnp.clip(1.0 + 0.1 * jax.random.normal(seeds[10], (DIN,), jnp.float32), 0.5, 1.5)
    out_weight = normal_values(seeds[11], (DIN, D), DIN ** -0.5, 0.1875, ((0, 4),))
    head_weight = draw_head_weight(jax.random.fold_in(seeds[13], 71), part)
    return {"patches": patches, "labels": labels, "op_ids": op_ids, "mix_codes": mix_codes, "aug_gains": aug_gains, "in_weight": in_weight, "dt_weight": dt_weight, "dt_bias": dt_bias, "decay_log": decay_log, "skip_gain": skip_gain, "norm_gain": norm_gain, "out_weight": out_weight, "head_weight": head_weight}


loss_scale = 256.0
mix_lambda = 12.0
highest = lax.Precision.HIGHEST

def view_scales(op_ids, mix_codes, aug_gains):
    code_values = mix_codes.astype(jnp.float32)
    weights = code_values[:, :WIDTH_AUG] / lax.optimization_barrier(jnp.sum(code_values[:, :WIDTH_AUG], axis=1, keepdims=True))
    keep_share = code_values[:, WIDTH_AUG] / 9.0
    onehot = (op_ids[:, :, None] == jnp.arange(NOPS, dtype=jnp.int32)[None, None, :]).astype(jnp.float32)
    op_weights = lax.optimization_barrier(jnp.sum(onehot * weights[:, :, None], axis=1))
    mixed_gain = jnp.dot(op_weights, aug_gains, precision=highest)
    scaled = keep_share[:, None] + (1.0 - keep_share[:, None]) * mixed_gain
    return jnp.concatenate([jnp.ones((1, D), jnp.float32), scaled], axis=0)

def block_pass(values, write_vectors, read_vectors, step_sizes, decay_rates):
    length = values.shape[0]
    pieces = length // BLOCK
    shaped = (values.reshape(pieces, BLOCK, HEADS, HEAD_DIM), write_vectors.reshape(pieces, BLOCK, STATE), read_vectors.reshape(pieces, BLOCK, STATE), step_sizes.reshape(pieces, BLOCK, HEADS))
    lower_mask = jnp.arange(BLOCK)[:, None] >= jnp.arange(BLOCK)[None, :]

    def advance(carried_in, inputs):
        state_now, offset = carried_in
        piece_values, piece_write, piece_read, piece_steps = inputs
        value_float = piece_values.astype(jnp.float32)
        write_float = piece_write.astype(jnp.float32)
        read_float = piece_read.astype(jnp.float32)
        step_logs = piece_steps * decay_rates[None, :]
        running = jnp.cumsum(step_logs, axis=0)
        log_gaps = running[:, None, :] - running[None, :, :]
        mask_decay = jnp.exp(jnp.where(lower_mask[:, :, None], log_gaps, -1e+30))
        scores = jnp.dot(read_float, write_float.T, precision=highest)
        mixing = scores[:, :, None] * mask_decay * piece_steps[None, :, :]
        inside = jnp.einsum('tsh,shp->thp', mixing, value_float, precision=highest)
        carried = jnp.exp(running)[:, :, None] * jnp.einsum('tn,hpn->thp', read_float, state_now, precision=highest)
        last_log = running[-1]
        weighted = (jnp.exp(last_log[None, :] - running) * piece_steps)[:, :, None] * value_float
        new_state = jnp.exp(last_log)[:, None, None] * state_now + jnp.einsum('shp,sn->hpn', weighted, write_float, precision=highest)
        return ((new_state, offset + last_log), (inside + carried, offset[None, :] + running))
    initial = (jnp.zeros((HEADS, HEAD_DIM, STATE), jnp.float32), jnp.zeros((HEADS,), jnp.float32))
    (final_state, total_log), (outputs, positions_log) = lax.scan(advance, initial, shaped)
    return (outputs.reshape(length, HEADS, HEAD_DIM), positions_log.reshape(length, HEADS), final_state, total_log)

def loss_terms(logits, labels):
    log_probs = jax.nn.log_softmax(logits, axis=-1)
    probabilities = jnp.exp(log_probs)
    log_mean = jax.scipy.special.logsumexp(log_probs, axis=0) - jnp.log(jnp.float32(VIEWS))
    spread = lax.optimization_barrier(jnp.sum(probabilities * (log_probs - log_mean[None]), axis=(0, 2))) / VIEWS
    onehot = (labels[:, None] == jnp.arange(CLASSES, dtype=jnp.int32)[None, :]).astype(jnp.float32)
    cross_entropy = -lax.optimization_barrier(jnp.sum(onehot * log_probs[0], axis=-1))
    return cross_entropy + mix_lambda * spread

def reference(patches, labels, op_ids, mix_codes, aug_gains, in_weight, dt_weight, dt_bias, decay_log, skip_gain, norm_gain, out_weight, head_weight):
    scales = view_scales(op_ids, mix_codes, aug_gains)
    views = (scales[:, None, :] * patches.astype(jnp.float32)[None]).astype(jnp.bfloat16)
    flat_rows = views.reshape(VIEWS * PATCHES, D)
    projected = jnp.dot(flat_rows, in_weight, preferred_element_type=jnp.float32).astype(jnp.bfloat16)
    projected = projected.reshape(VIEWS, PATCHES, PROJ)
    raw_steps = jnp.dot(flat_rows, dt_weight, preferred_element_type=jnp.float32).reshape(VIEWS, PATCHES, 2, HEADS)
    step_sizes = jax.nn.softplus(raw_steps + dt_bias[None, None])
    decay_rates = -jnp.exp(decay_log)
    values = projected[:, :, :DIN].reshape(VIEWS, PATCHES, HEADS, HEAD_DIM)
    coefficients = projected[:, :, DIN:].reshape(VIEWS, PATCHES, 4, STATE)
    mapped = jax.vmap(block_pass, in_axes=(0, 0, 0, 0, None))
    forward_out = mapped(values, coefficients[:, :, 0], coefficients[:, :, 1], step_sizes[:, :, 0], decay_rates[0])[0]
    reverse_out = mapped(jnp.flip(values, 1), jnp.flip(coefficients[:, :, 2], 1), jnp.flip(coefficients[:, :, 3], 1), jnp.flip(step_sizes[:, :, 1], 1), decay_rates[1])[0]
    mixed = forward_out + jnp.flip(reverse_out, 1) + skip_gain[None, None, :, None] * values.astype(jnp.float32)
    mixed = mixed.reshape(VIEWS * PATCHES, DIN)
    normed = (mixed * lax.rsqrt(lax.optimization_barrier(jnp.mean(mixed * mixed, axis=-1, keepdims=True)) + 1e-05) * norm_gain[None, :]).astype(jnp.bfloat16)
    hidden = (flat_rows.astype(jnp.float32) + jnp.dot(normed, out_weight, preferred_element_type=jnp.float32)).astype(jnp.bfloat16)
    logits = jnp.dot(hidden, head_weight, preferred_element_type=jnp.float32).reshape(VIEWS, PATCHES, CLASSES)

    def per_patch(logit_values):
        return loss_terms(logit_values, labels)
    patch_loss, pullback = jax.vjp(per_patch, logits)
    grad_logits, = pullback(jnp.full((PATCHES,), loss_scale / PATCHES, jnp.float32))
    grad_logits_bf = grad_logits.reshape(VIEWS * PATCHES, CLASSES).astype(jnp.bfloat16)
    grad_hidden = lax.dot_general(grad_logits_bf, head_weight, (((1,), (1,)), ((), ())), preferred_element_type=jnp.float32).astype(jnp.bfloat16)
    grad_out = lax.dot_general(normed, grad_hidden, (((0,), (0,)), ((), ())), preferred_element_type=jnp.float32)
    grad_head = lax.dot_general(hidden, grad_logits_bf, (((0,), (0,)), ((), ())), preferred_element_type=jnp.float32)
    return (grad_out, grad_head, patch_loss)
```

```python
import functools
import jax
import jax.numpy as jnp
from jax import lax
from jax.experimental import pallas as pl
from jax.experimental.pallas import tpu as pltpu
from jax.sharding import PartitionSpec as P

D = 1024
HEADS = 16
HEAD_DIM = 64
STATE = 128
CLASSES = 128
VIEWS = 3
NOPS = 9
WIDTH_AUG = 3
BLOCK = 128
LANES = 128
LOG_ROWS = 8


loss_scale = 256.0
mix_lambda = 12.0
highest = lax.Precision.HIGHEST
f32 = jnp.float32
bf16 = jnp.bfloat16


def view_scales(op_ids, mix_codes, aug_gains):
    code_values = mix_codes.astype(jnp.float32)
    weights = code_values[:, :WIDTH_AUG] / jnp.sum(
        code_values[:, :WIDTH_AUG], axis=1, keepdims=True
    )
    keep_share = code_values[:, WIDTH_AUG] / 9.0
    onehot = (op_ids[:, :, None] == jnp.arange(NOPS, dtype=jnp.int32)[None, None, :]).astype(
        jnp.float32
    )
    op_weights = jnp.sum(onehot * weights[:, :, None], axis=1)
    mixed_gain = jnp.dot(op_weights, aug_gains, precision=highest)
    scaled = keep_share[:, None] + (1.0 - keep_share[:, None]) * mixed_gain
    return jnp.concatenate([jnp.ones((1, D), jnp.float32), scaled], axis=0)


def halves(value):
    high = value.astype(bf16)
    return high, (value - high.astype(f32)).astype(bf16)


def thirds(value):
    high = value.astype(bf16)
    rest = value - high.astype(f32)
    mid = rest.astype(bf16)
    return high, mid, (rest - mid.astype(f32)).astype(bf16)


def dot(a, b, dims=((1,), (0,))):
    return lax.dot_general(a, b, (dims, ((), ())), preferred_element_type=f32)


def spread(columns, first, heads):
    rows = columns.shape[0]
    lane = lax.broadcasted_iota(jnp.int32, (rows, LANES), 1)
    pieces = []
    for h in range(first, first + heads, 2):
        left = jnp.broadcast_to(columns[:, h : h + 1], (rows, LANES))
        right = jnp.broadcast_to(columns[:, h + 1 : h + 2], (rows, LANES))
        pieces.append(jnp.where(lane < HEAD_DIM, left, right))
    return jnp.concatenate(pieces, axis=1) if len(pieces) > 1 else pieces[0]


def states_kernel(heads, raw_ref, x_ref, coef_ref, bias_ref, rate_ref,
                  final_ref, prefix_ref, steps_ref, run_ref, pos_ref):
    rows, width = x_ref.shape[1:]
    pieces = rows // BLOCK
    row = lax.broadcasted_iota(jnp.int32, (BLOCK, BLOCK), 0)
    col = lax.broadcasted_iota(jnp.int32, (BLOCK, BLOCK), 1)
    lower = (row >= col).astype(f32).astype(bf16)
    upper = (row <= col).astype(f32).astype(bf16)
    is_forward = col < heads

    def first_pass(i, carried):
        state, total = carried
        at = pl.ds(pl.multiple_of(i * BLOCK, BLOCK), BLOCK)
        raw = raw_ref[0, at, :] + bias_ref[...]
        steps = jnp.maximum(raw, 0.0) + jnp.log1p(jnp.exp(-jnp.abs(raw)))
        parts = thirds(steps * rate_ref[...])
        down = sum(dot(lower, part) for part in parts)
        up = sum(dot(upper, part) for part in parts)
        run = jnp.where(is_forward, down, up)
        steps_ref[0, at, :] = steps
        run_ref[0, at, :] = run
        pos_ref[0, at, :] = run + total
        last = jnp.where(is_forward[:1], run[BLOCK - 1 :], run[:1])
        x = x_ref[0, at, :].astype(f32)
        weight = spread(jnp.exp(last - run) * steps, 0, heads)
        high, low = halves(weight * x)
        write = coef_ref[0, at, :STATE]
        fresh = dot(write, high, ((0,), (0,))) + dot(write, low, ((0,), (0,)))
        s_high, s_low = halves(state)
        prefix_ref[0, 0, i, :STATE, :] = s_high
        prefix_ref[0, 0, i, STATE:, :] = s_low
        return spread(jnp.exp(last), 0, heads) * state + fresh, total + last

    zero = jnp.zeros((STATE, width), f32)
    no_log = jnp.zeros((1, LANES), f32)
    state, total = lax.fori_loop(0, pieces, first_pass, (zero, no_log))
    final_ref[0, 0, :STATE, :] = state
    final_ref[0, 0, STATE:, :] = jnp.broadcast_to(spread(total, 0, heads), (LOG_ROWS, width))

    def second_pass(k, carried):
        state, total = carried
        i = pieces - 1 - k
        at = pl.ds(pl.multiple_of(i * BLOCK, BLOCK), BLOCK)
        run = run_ref[0, at, :]
        last = run[:1]
        pos_ref[0, at, :] = jnp.where(is_forward, pos_ref[0, at, :], run + total)
        x = x_ref[0, at, :].astype(f32)
        weight = spread(jnp.exp(last - run) * steps_ref[0, at, :], heads, heads)
        high, low = halves(weight * x)
        write = coef_ref[0, at, 2 * STATE : 3 * STATE]
        fresh = dot(write, high, ((0,), (0,))) + dot(write, low, ((0,), (0,)))
        s_high, s_low = halves(state)
        prefix_ref[0, 1, i, :STATE, :] = s_high
        prefix_ref[0, 1, i, STATE:, :] = s_low
        return spread(jnp.exp(last), heads, heads) * state + fresh, total + last

    state, total = lax.fori_loop(0, pieces, second_pass, (zero, no_log))
    final_ref[0, 1, :STATE, :] = state
    final_ref[0, 1, STATE:, :] = jnp.broadcast_to(spread(total, heads, heads), (LOG_ROWS, width))


def inside_kernel(heads, x_ref, coef_ref, prefix_ref, steps_ref, run_ref, skip_ref, out_ref):
    row = lax.broadcasted_iota(jnp.int32, (BLOCK, BLOCK), 0)
    col = lax.broadcasted_iota(jnp.int32, (BLOCK, BLOCK), 1)
    below, above = row > col, row < col
    x = x_ref[0]
    steps_t = steps_ref[0].T
    run = run_ref[0]
    run_t = run.T
    coef = coef_ref[0]
    write_f, read_f = coef[:, :STATE], coef[:, STATE : 2 * STATE]
    write_r, read_r = coef[:, 2 * STATE : 3 * STATE], coef[:, 3 * STATE :]
    score_f = dot(read_f, write_f, ((1,), (1,)))
    score_r = dot(read_r, write_r, ((1,), (1,)))
    lane = lax.broadcasted_iota(jnp.int32, (BLOCK, LANES), 1)
    zero = jnp.zeros((BLOCK, LANES), bf16)
    pieces = []
    for pair in range(heads // 2):
        highs, lows = [], []
        for h in (2 * pair, 2 * pair + 1):
            r = heads + h
            gap = jnp.where(
                below, run[:, h : h + 1] - run_t[h : h + 1], run[:, r : r + 1] - run_t[r : r + 1]
            )
            gap = jnp.where(row == col, 0.0, gap)
            from_f = score_f * steps_t[h : h + 1]
            from_r = score_r * steps_t[r : r + 1]
            weight = jnp.where(below, from_f, jnp.where(above, from_r, from_f + from_r))
            high, low = halves(weight * jnp.exp(gap))
            highs.append(high)
            lows.append(low)
        values = x[:, pair * LANES : (pair + 1) * LANES]
        stacked = jnp.concatenate(
            [jnp.where(lane < HEAD_DIM, values, zero), jnp.where(lane < HEAD_DIM, zero, values)],
            axis=0,
        )
        pieces.append(
            dot(jnp.concatenate(highs, axis=1), stacked)
            + dot(jnp.concatenate(lows, axis=1), stacked)
        )
    inside = jnp.concatenate(pieces, axis=1) if len(pieces) > 1 else pieces[0]
    grown = jnp.exp(run)
    carried_f = dot(jnp.concatenate([read_f, read_f], axis=1), prefix_ref[0, 0, 0])
    carried_r = dot(jnp.concatenate([read_r, read_r], axis=1), prefix_ref[0, 1, 0])
    out_ref[0] = (
        inside
        + spread(grown, 0, heads) * carried_f
        + spread(grown, heads, heads) * carried_r
        + skip_ref[...] * x.astype(f32)
    )


def incoming_kernel(heads, count, mine_ref, states_ref, coef_ref, pos_ref, local_ref,
                    mixed_ref, square_ref, held):
    width = local_ref.shape[2]
    mine = mine_ref[0]

    @pl.when(pl.program_id(1) == 0)
    def _():
        for way in range(2):
            before = jnp.zeros((STATE, width), f32)
            for k in range(count):
                at = k if way == 0 else count - 1 - k
                decay = jnp.exp(states_ref[at, 0, way, STATE : STATE + 1, :])
                new = decay * before + states_ref[at, 0, way, :STATE, :]
                reached = (at < mine) if way == 0 else (at > mine)
                before = jnp.where(reached, new, before)
            high, low = halves(before)
            held[way, :STATE, :] = high
            held[way, STATE:, :] = low

    grown = jnp.exp(pos_ref[0])
    coef = coef_ref[0]
    read_f = coef[:, STATE : 2 * STATE]
    read_r = coef[:, 3 * STATE :]
    mixed = (
        local_ref[0]
        + spread(grown, 0, heads) * dot(jnp.concatenate([read_f, read_f], axis=1), held[0])
        + spread(grown, heads, heads) * dot(jnp.concatenate([read_r, read_r], axis=1), held[1])
    )
    mixed_ref[0] = mixed
    ones = jnp.ones((8, width), bf16)
    square_ref[0] = sum(dot(ones, part, ((1,), (1,))) for part in thirds(mixed * mixed))


def tail_kernel(shards, factor, normed_ref, out_w_ref, head_ref, patches_ref, scale_ref,
                label_ref, logit_ref, loss_ref, head_grad_ref, hidden_ref=None):
    rows = patches_ref.shape[0]
    head = head_ref[...]
    patches = patches_ref[...].astype(f32)
    hiddens, logs = [], []
    for v in range(VIEWS):
        total = dot(normed_ref[0, v], out_w_ref[0])
        for s in range(1, shards):
            total += dot(normed_ref[s, v], out_w_ref[s])
        view = (scale_ref[v : v + 1, :] * patches).astype(bf16)
        hidden = (view.astype(f32) + total).astype(bf16)
        hiddens.append(hidden)
        logits = dot(hidden, head)
        shifted = logits - jnp.max(logits, axis=1, keepdims=True)
        logs.append(shifted - jnp.log(jnp.sum(jnp.exp(shifted), axis=1, keepdims=True)))
    top = jnp.maximum(jnp.maximum(logs[0], logs[1]), logs[2])
    mean = top + jnp.log(sum(jnp.exp(log - top) for log in logs)) - jnp.log(f32(VIEWS))
    lane = lax.broadcasted_iota(jnp.int32, (rows, CLASSES), 1)
    onehot = (lane == label_ref[...]).astype(f32)
    spread_sum = jnp.zeros((rows, 1), f32)
    grads = []
    for v in range(VIEWS):
        prob = jnp.exp(logs[v])
        gap = logs[v] - mean
        inner = jnp.sum(prob * gap, axis=1, keepdims=True)
        spread_sum += inner
        grad = (mix_lambda / VIEWS) * prob * (gap - inner)
        if v == 0:
            grad += prob - onehot
        grads.append((factor * grad).astype(bf16))
        logit_ref[v] = grads[v]
    cross = -jnp.sum(onehot * logs[0], axis=1, keepdims=True)
    loss_ref[...] = cross + mix_lambda * (spread_sum / VIEWS)
    update = sum(dot(hiddens[v], grads[v], ((0,), (0,))) for v in range(VIEWS))

    @pl.when(pl.program_id(0) == 0)
    def _():
        head_grad_ref[...] = update

    @pl.when(pl.program_id(0) > 0)
    def _():
        head_grad_ref[...] += update


def grad_kernel(shards, normed_ref, logit_ref, head_ref, out_ref):
    grads = logit_ref[0, 0]
    hidden = dot(grads, head_ref[...], ((1,), (1,))).astype(bf16)
    update = dot(normed_ref[0], hidden, ((0,), (0,)))
    first = (pl.program_id(0) == 0) & (pl.program_id(1) == 0)

    @pl.when(first)
    def _():
        out_ref[...] = update

    @pl.when(jnp.logical_not(first))
    def _():
        out_ref[...] += update


def call(kernel, name, flops, moved, limit=48 << 20, **options):
    return pl.pallas_call(
        kernel,
        name=name,
        compiler_params=pltpu.CompilerParams(vmem_limit_bytes=limit),
        cost_estimate=pl.CostEstimate(flops=flops, bytes_accessed=moved, transcendentals=0),
        **options,
    )


def own(columns, place, shards, heads, width):
    shaped = columns.reshape(columns.shape[0], heads, shards, width)
    return lax.dynamic_index_in_dim(shaped, place, 2, False).reshape(-1, heads * width)


def on_device(
    patches,
    labels,
    op_ids,
    mix_codes,
    aug_gains,
    in_weight,
    dt_weight,
    dt_bias,
    decay_log,
    skip_gain,
    norm_gain,
    out_weight,
    head_weight,
):
    row_count = patches.shape[0]
    ctx_count = lax.axis_size("ctx")
    shards = lax.axis_size("fsdp")
    place = lax.axis_index("fsdp")
    total_patches = row_count * ctx_count * shards
    inner = out_weight.shape[0] * shards
    heads = HEADS // shards
    width = heads * HEAD_DIM
    rows = row_count * shards
    pieces = rows // BLOCK

    patches_all = lax.all_gather(patches, "fsdp", axis=0, tiled=True)
    weights = lax.all_gather(
        jnp.concatenate([in_weight, dt_weight], axis=1), "fsdp", axis=0, tiled=True
    )
    out_all = lax.all_gather(out_weight, "fsdp", axis=0, tiled=True)
    columns_in = inner + 4 * STATE
    step_columns = weights[:, columns_in:].reshape(D, 2 * heads, shards)
    step_columns = lax.dynamic_index_in_dim(step_columns, place, 2, False)
    mine_weight = jnp.concatenate(
        [
            own(weights[:, :inner], place, shards, heads, HEAD_DIM),
            weights[:, inner:columns_in],
            step_columns,
            jnp.zeros((D, LANES - 2 * heads), bf16),
        ],
        axis=1,
    )
    scales = view_scales(op_ids, mix_codes, aug_gains)
    views = (scales[:, None, :] * patches_all.astype(f32)[None]).astype(bf16)
    projected = dot(views.reshape(VIEWS * rows, D), mine_weight)
    projected = projected.reshape(VIEWS, rows, width + 5 * STATE)
    x = projected[:, :, :width].astype(bf16)
    coef = projected[:, :, width : width + 4 * STATE].astype(bf16)
    raw = projected[:, :, width + 4 * STATE :]

    def local_lanes(values):
        picked = lax.dynamic_index_in_dim(values.reshape(2 * heads, shards), place, 1, False)
        return jnp.pad(picked, (0, LANES - 2 * heads))[None, :]

    bias = local_lanes(dt_bias)
    rate = local_lanes(-jnp.exp(decay_log))
    skip = lax.dynamic_index_in_dim(skip_gain.reshape(heads, shards), place, 1, False)
    skip = jnp.repeat(skip, HEAD_DIM)[None, :]
    gain = own(norm_gain[None, :], place, shards, heads, HEAD_DIM)

    whole = lambda *dims: pl.BlockSpec((1, *dims), lambda v: (v,) + (0,) * len(dims))
    fixed = lambda *dims: pl.BlockSpec(dims, lambda *_: (0,) * len(dims))
    final, prefix, steps, run, pos = call(
        functools.partial(states_kernel, heads), "states",
        VIEWS * rows * STATE * width * 8, VIEWS * rows * 8192,
        grid=(VIEWS,),
        in_specs=[whole(rows, LANES), whole(rows, width), whole(rows, 4 * STATE),
                  fixed(1, LANES), fixed(1, LANES)],
        out_specs=[whole(2, STATE + LOG_ROWS, width), whole(2, pieces, 2 * STATE, width),
                   whole(rows, LANES), whole(rows, LANES), whole(rows, LANES)],
        out_shape=[
            jax.ShapeDtypeStruct((VIEWS, 2, STATE + LOG_ROWS, width), f32),
            jax.ShapeDtypeStruct((VIEWS, 2, pieces, 2 * STATE, width), bf16),
            jax.ShapeDtypeStruct((VIEWS, rows, LANES), f32),
            jax.ShapeDtypeStruct((VIEWS, rows, LANES), f32),
            jax.ShapeDtypeStruct((VIEWS, rows, LANES), f32),
        ],
    )(raw, x, coef, bias, rate)
    everything = lax.all_gather(final, "ctx")

    block = lambda *dims: pl.BlockSpec((1, *dims), lambda v, i: (v, i) + (0,) * (len(dims) - 1))
    local = call(
        functools.partial(inside_kernel, heads), "inside",
        VIEWS * rows * STATE * width * 16, VIEWS * rows * 8192,
        grid=(VIEWS, pieces),
        in_specs=[block(BLOCK, width), block(BLOCK, 4 * STATE),
                  pl.BlockSpec((1, 2, 1, 2 * STATE, width), lambda v, i: (v, 0, i, 0, 0)),
                  block(BLOCK, LANES), block(BLOCK, LANES), fixed(1, width)],
        out_specs=block(BLOCK, width),
        out_shape=jax.ShapeDtypeStruct((VIEWS, rows, width), f32),
    )(x, coef, prefix, steps, run, skip)

    span = min(rows, 512)
    mixed, squares = call(
        functools.partial(incoming_kernel, heads, ctx_count), "incoming",
        VIEWS * rows * STATE * width * 8, VIEWS * rows * 8192,
        grid=(VIEWS, rows // span),
        in_specs=[
            pl.BlockSpec(memory_space=pltpu.SMEM),
            pl.BlockSpec((ctx_count, 1, 2, STATE + LOG_ROWS, width), lambda v, i: (0, v, 0, 0, 0)),
            block(span, 4 * STATE), block(span, LANES), block(span, width)],
        out_specs=[block(span, width), pl.BlockSpec((1, 8, span), lambda v, i: (v, 0, i))],
        out_shape=[
            jax.ShapeDtypeStruct((VIEWS, rows, width), f32),
            jax.ShapeDtypeStruct((VIEWS, 8, rows), f32),
        ],
        scratch_shapes=[pltpu.VMEM((2, 2 * STATE, width), bf16)],
    )(lax.axis_index("ctx").reshape(1), everything, coef, pos, local)

    square_total = lax.psum(squares[:, 0, :], "fsdp")
    scaling = lax.rsqrt(square_total / inner + 1e-05)
    normed = (mixed * scaling[:, :, None] * gain[None]).astype(bf16)
    outgoing = normed.reshape(VIEWS, shards, row_count, width).transpose(1, 0, 2, 3)
    arrived = lax.all_to_all(outgoing, "fsdp", split_axis=0, concat_axis=0)

    out_own = out_all.reshape(heads, shards, HEAD_DIM, D).transpose(1, 0, 2, 3)
    out_own = out_own.reshape(shards, width, D)
    tile = min(row_count, 128)
    grads, losses, head_term = call(
        functools.partial(tail_kernel, shards, loss_scale / total_patches), "tail",
        VIEWS * row_count * D * 3000, 6 << 20,
        grid=(row_count // tile,),
        in_specs=[
            pl.BlockSpec((shards, VIEWS, tile, width), lambda i: (0, 0, i, 0)),
            fixed(shards, width, D), fixed(D, CLASSES),
            pl.BlockSpec((tile, D), lambda i: (i, 0)),
            fixed(VIEWS, D),
            pl.BlockSpec((tile, 1), lambda i: (i, 0))],
        out_specs=[
            pl.BlockSpec((VIEWS, tile, CLASSES), lambda i: (0, i, 0)),
            pl.BlockSpec((tile, 1), lambda i: (i, 0)),
            fixed(D, CLASSES)],
        out_shape=[
            jax.ShapeDtypeStruct((VIEWS, row_count, CLASSES), bf16),
            jax.ShapeDtypeStruct((row_count, 1), f32),
            jax.ShapeDtypeStruct((D, CLASSES), f32),
        ],
    )(arrived, out_own, head_weight, patches, scales, labels[:, None])

    if ctx_count * shards == HEADS:
        grads_all = lax.all_gather(grads, "fsdp")
        grad_rows = call(
            functools.partial(grad_kernel, shards), "grads",
            VIEWS * rows * D * (width + CLASSES) * 2, 8 << 20,
            grid=(VIEWS, shards),
            in_specs=[
                pl.BlockSpec((1, row_count, width), lambda v, s: (v, s, 0)),
                pl.BlockSpec((1, 1, row_count, CLASSES), lambda v, s: (s, v, 0, 0)),
                fixed(D, CLASSES)],
            out_specs=fixed(width, D),
            out_shape=jax.ShapeDtypeStruct((width, D), f32),
        )(normed, grads_all, head_weight)
        grad_out = lax.psum_scatter(grad_rows, "ctx", scatter_dimension=0, tiled=True)
    else:
        grad_hidden = lax.dot_general(
            grads, head_weight, (((2,), (1,)), ((), ())), preferred_element_type=f32
        ).astype(bf16)
        grad_rows = lax.dot_general(
            arrived, grad_hidden, (((1, 2), (0, 1)), ((), ())), preferred_element_type=f32
        )
        grad_rows = grad_rows.reshape(shards, heads, HEAD_DIM, D).transpose(1, 0, 2, 3)
        grad_out = lax.psum_scatter(
            grad_rows.reshape(inner, D), ("ctx", "fsdp"), scatter_dimension=0, tiled=True
        )
    grad_head = lax.psum_scatter(head_term, ("ctx", "fsdp"), scatter_dimension=0, tiled=True)
    return (grad_out, grad_head, losses[:, 0])


def solution(mesh):
    return jax.shard_map(
        on_device,
        mesh=mesh,
        in_specs=(
            P(("groups", "ctx", "fsdp"), None),
            P(("groups", "ctx", "fsdp")),
            P("groups", None),
            P("groups", None),
            P(),
            P("fsdp", None),
            P("fsdp", None),
            P(),
            P(),
            P(),
            P(),
            P("fsdp", None),
            P(),
        ),
        out_specs=(
            P(("groups", "ctx", "fsdp"), None),
            P(("groups", "ctx", "fsdp"), None),
            P(("groups", "ctx", "fsdp")),
        ),
        check_vma=False,
    )
```

```python
import functools
import jax
import jax.numpy as jnp
from jax import lax
from jax.experimental import pallas as pl
from jax.experimental.pallas import tpu as pltpu
from jax.sharding import PartitionSpec as P

D = 1024
HEADS = 16
HEAD_DIM = 64
STATE = 128
CLASSES = 128
VIEWS = 3
NOPS = 9
WIDTH_AUG = 3
BLOCK = 128
LANES = 128
LOG_ROWS = 8


loss_scale = 256.0
mix_lambda = 12.0
highest = lax.Precision.HIGHEST
f32 = jnp.float32
bf16 = jnp.bfloat16


def view_scales(op_ids, mix_codes, aug_gains):
    code_values = mix_codes.astype(jnp.float32)
    weights = code_values[:, :WIDTH_AUG] / jnp.sum(
        code_values[:, :WIDTH_AUG], axis=1, keepdims=True
    )
    keep_share = code_values[:, WIDTH_AUG] / 9.0
    onehot = (op_ids[:, :, None] == jnp.arange(NOPS, dtype=jnp.int32)[None, None, :]).astype(
        jnp.float32
    )
    op_weights = jnp.sum(onehot * weights[:, :, None], axis=1)
    mixed_gain = jnp.dot(op_weights, aug_gains, precision=highest)
    scaled = keep_share[:, None] + (1.0 - keep_share[:, None]) * mixed_gain
    return jnp.concatenate([jnp.ones((1, D), jnp.float32), scaled], axis=0)


def halves(value):
    high = value.astype(bf16)
    return high, (value - high.astype(f32)).astype(bf16)


def thirds(value):
    high = value.astype(bf16)
    rest = value - high.astype(f32)
    mid = rest.astype(bf16)
    return high, mid, (rest - mid.astype(f32)).astype(bf16)


def dot(a, b, dims=((1,), (0,))):
    return lax.dot_general(a, b, (dims, ((), ())), preferred_element_type=f32)


def spread(columns, first, heads):
    rows = columns.shape[0]
    lane = lax.broadcasted_iota(jnp.int32, (rows, LANES), 1)
    pieces = []
    for h in range(first, first + heads, 2):
        left = jnp.broadcast_to(columns[:, h : h + 1], (rows, LANES))
        right = jnp.broadcast_to(columns[:, h + 1 : h + 2], (rows, LANES))
        pieces.append(jnp.where(lane < HEAD_DIM, left, right))
    return jnp.concatenate(pieces, axis=1) if len(pieces) > 1 else pieces[0]


def states_kernel(heads, raw_ref, x_ref, coef_ref, bias_ref, rate_ref,
                  final_ref, prefix_ref, steps_ref, run_ref, pos_ref):
    rows, width = x_ref.shape[1:]
    pieces = rows // BLOCK
    row = lax.broadcasted_iota(jnp.int32, (BLOCK, BLOCK), 0)
    col = lax.broadcasted_iota(jnp.int32, (BLOCK, BLOCK), 1)
    lower = (row >= col).astype(f32).astype(bf16)
    upper = (row <= col).astype(f32).astype(bf16)
    is_forward = col < heads

    def first_pass(i, carried):
        state, total = carried
        at = pl.ds(pl.multiple_of(i * BLOCK, BLOCK), BLOCK)
        raw = raw_ref[0, at, :] + bias_ref[...]
        steps = jnp.maximum(raw, 0.0) + jnp.log1p(jnp.exp(-jnp.abs(raw)))
        parts = thirds(steps * rate_ref[...])
        down = sum(dot(lower, part) for part in parts)
        up = sum(dot(upper, part) for part in parts)
        run = jnp.where(is_forward, down, up)
        steps_ref[0, at, :] = steps
        run_ref[0, at, :] = run
        pos_ref[0, at, :] = run + total
        last = jnp.where(is_forward[:1], run[BLOCK - 1 :], run[:1])
        x = x_ref[0, at, :].astype(f32)
        weight = spread(jnp.exp(last - run) * steps, 0, heads)
        high, low = halves(weight * x)
        write = coef_ref[0, at, :STATE]
        fresh = dot(write, high, ((0,), (0,))) + dot(write, low, ((0,), (0,)))
        s_high, s_low = halves(state)
        prefix_ref[0, 0, i, :STATE, :] = s_high
        prefix_ref[0, 0, i, STATE:, :] = s_low
        return spread(jnp.exp(last), 0, heads) * state + fresh, total + last

    zero = jnp.zeros((STATE, width), f32)
    no_log = jnp.zeros((1, LANES), f32)
    state, total = lax.fori_loop(0, pieces, first_pass, (zero, no_log), unroll=4)
    final_ref[0, 0, :STATE, :] = state
    final_ref[0, 0, STATE:, :] = jnp.broadcast_to(spread(total, 0, heads), (LOG_ROWS, width))

    def second_pass(k, carried):
        state, total = carried
        i = pieces - 1 - k
        at = pl.ds(pl.multiple_of(i * BLOCK, BLOCK), BLOCK)
        run = run_ref[0, at, :]
        last = run[:1]
        pos_ref[0, at, :] = jnp.where(is_forward, pos_ref[0, at, :], run + total)
        x = x_ref[0, at, :].astype(f32)
        weight = spread(jnp.exp(last - run) * steps_ref[0, at, :], heads, heads)
        high, low = halves(weight * x)
        write = coef_ref[0, at, 2 * STATE : 3 * STATE]
        fresh = dot(write, high, ((0,), (0,))) + dot(write, low, ((0,), (0,)))
        s_high, s_low = halves(state)
        prefix_ref[0, 1, i, :STATE, :] = s_high
        prefix_ref[0, 1, i, STATE:, :] = s_low
        return spread(jnp.exp(last), heads, heads) * state + fresh, total + last

    state, total = lax.fori_loop(0, pieces, second_pass, (zero, no_log), unroll=4)
    final_ref[0, 1, :STATE, :] = state
    final_ref[0, 1, STATE:, :] = jnp.broadcast_to(spread(total, heads, heads), (LOG_ROWS, width))


def inside_kernel(heads, x_ref, coef_ref, prefix_ref, steps_ref, run_ref, skip_ref, *rest):
    out_ref = rest[-1]
    row = lax.broadcasted_iota(jnp.int32, (BLOCK, BLOCK), 0)
    col = lax.broadcasted_iota(jnp.int32, (BLOCK, BLOCK), 1)
    below, above = row > col, row < col
    x = x_ref[0]
    steps_t = steps_ref[0].T
    run = run_ref[0]
    run_t = run.T
    coef = coef_ref[0]
    write_f, read_f = coef[:, :STATE], coef[:, STATE : 2 * STATE]
    write_r, read_r = coef[:, 2 * STATE : 3 * STATE], coef[:, 3 * STATE :]
    score_f = dot(read_f, write_f, ((1,), (1,)))
    score_r = dot(read_r, write_r, ((1,), (1,)))
    lane = lax.broadcasted_iota(jnp.int32, (BLOCK, LANES), 1)
    zero = jnp.zeros((BLOCK, LANES), bf16)
    pieces = []
    for pair in range(heads // 2):
        highs, lows = [], []
        for h in (2 * pair, 2 * pair + 1):
            r = heads + h
            gap = jnp.where(
                below, run[:, h : h + 1] - run_t[h : h + 1], run[:, r : r + 1] - run_t[r : r + 1]
            )
            gap = jnp.where(row == col, 0.0, gap)
            from_f = score_f * steps_t[h : h + 1]
            from_r = score_r * steps_t[r : r + 1]
            weight = jnp.where(below, from_f, jnp.where(above, from_r, from_f + from_r))
            high, low = halves(weight * jnp.exp(gap))
            highs.append(high)
            lows.append(low)
        values = x[:, pair * LANES : (pair + 1) * LANES]
        stacked = jnp.concatenate(
            [jnp.where(lane < HEAD_DIM, values, zero), jnp.where(lane < HEAD_DIM, zero, values)],
            axis=0,
        )
        pieces.append(
            dot(jnp.concatenate(highs, axis=1), stacked)
            + dot(jnp.concatenate(lows, axis=1), stacked)
        )
    inside = jnp.concatenate(pieces, axis=1) if len(pieces) > 1 else pieces[0]
    grown = jnp.exp(run)
    carried_f = dot(jnp.concatenate([read_f, read_f], axis=1), prefix_ref[0, 0, 0])
    carried_r = dot(jnp.concatenate([read_r, read_r], axis=1), prefix_ref[0, 1, 0])
    out_ref[0] = (
        inside
        + spread(grown, 0, heads) * carried_f
        + spread(grown, heads, heads) * carried_r
        + skip_ref[...] * x.astype(f32)
    )


def incoming_kernel(heads, forward_ref, reverse_ref, coef_ref, pos_ref, local_ref,
                    mixed_ref, square_ref, held):
    width = local_ref.shape[2]

    @pl.when(pl.program_id(1) == 0)
    def _():
        for way, before in enumerate((forward_ref, reverse_ref)):
            high, low = halves(before[0])
            held[way, :STATE, :] = high
            held[way, STATE:, :] = low

    grown = jnp.exp(pos_ref[0])
    coef = coef_ref[0]
    read_f = coef[:, STATE : 2 * STATE]
    read_r = coef[:, 3 * STATE :]
    mixed = (
        local_ref[0]
        + spread(grown, 0, heads) * dot(jnp.concatenate([read_f, read_f], axis=1), held[0])
        + spread(grown, heads, heads) * dot(jnp.concatenate([read_r, read_r], axis=1), held[1])
    )
    mixed_ref[0] = mixed
    ones = jnp.ones((8, width), bf16)
    square_ref[0] = sum(dot(ones, part, ((1,), (1,))) for part in thirds(mixed * mixed))


def tail_kernel(shards, factor, normed_ref, out_w_ref, head_ref, patches_ref, scale_ref,
                label_ref, logit_ref, loss_ref, head_grad_ref, hidden_ref=None):
    rows = patches_ref.shape[0]
    head = head_ref[...]
    patches = patches_ref[...].astype(f32)
    hiddens, logs = [], []
    for v in range(VIEWS):
        total = dot(normed_ref[0, v], out_w_ref[0])
        for s in range(1, shards):
            total += dot(normed_ref[s, v], out_w_ref[s])
        view = (scale_ref[v : v + 1, :] * patches).astype(bf16)
        hidden = (view.astype(f32) + total).astype(bf16)
        hiddens.append(hidden)
        logits = dot(hidden, head)
        shifted = logits - jnp.max(logits, axis=1, keepdims=True)
        logs.append(shifted - jnp.log(jnp.sum(jnp.exp(shifted), axis=1, keepdims=True)))
    top = jnp.maximum(jnp.maximum(logs[0], logs[1]), logs[2])
    mean = top + jnp.log(sum(jnp.exp(log - top) for log in logs)) - jnp.log(f32(VIEWS))
    lane = lax.broadcasted_iota(jnp.int32, (rows, CLASSES), 1)
    onehot = (lane == label_ref[...]).astype(f32)
    spread_sum = jnp.zeros((rows, 1), f32)
    grads = []
    for v in range(VIEWS):
        prob = jnp.exp(logs[v])
        gap = logs[v] - mean
        inner = jnp.sum(prob * gap, axis=1, keepdims=True)
        spread_sum += inner
        grad = (mix_lambda / VIEWS) * prob * (gap - inner)
        if v == 0:
            grad += prob - onehot
        grads.append((factor * grad).astype(bf16))
        logit_ref[v] = grads[v]
    cross = -jnp.sum(onehot * logs[0], axis=1, keepdims=True)
    loss_ref[...] = cross + mix_lambda * (spread_sum / VIEWS)
    update = sum(dot(hiddens[v], grads[v], ((0,), (0,))) for v in range(VIEWS))

    @pl.when(pl.program_id(0) == 0)
    def _():
        head_grad_ref[...] = update

    @pl.when(pl.program_id(0) > 0)
    def _():
        head_grad_ref[...] += update


def grad_kernel(shards, normed_ref, logit_ref, head_ref, out_ref):
    grads = logit_ref[0, 0]
    hidden = dot(grads, head_ref[...], ((1,), (1,))).astype(bf16)
    update = dot(normed_ref[0], hidden, ((0,), (0,)))
    first = (pl.program_id(0) == 0) & (pl.program_id(1) == 0)

    @pl.when(first)
    def _():
        out_ref[...] = update

    @pl.when(jnp.logical_not(first))
    def _():
        out_ref[...] += update


def call(kernel, name, flops, moved, limit=48 << 20, **options):
    return pl.pallas_call(
        kernel,
        name=name,
        compiler_params=pltpu.CompilerParams(vmem_limit_bytes=limit),
        cost_estimate=pl.CostEstimate(flops=flops, bytes_accessed=moved, transcendentals=0),
        **options,
    )


def carried_in(state, decay, axis, reverse):
    count = lax.axis_size(axis)
    if reverse:
        hops = [(j, j - 1) for j in range(1, count)]
    else:
        hops = [(j, j + 1) for j in range(count - 1)]
    sent, got = state, jnp.zeros_like(state)
    for hop in range(count - 1):
        got = lax.ppermute(sent, axis, hops)
        sent = decay * got + state
    return got


def scatter_sum(terms, axes, count):
    blocks = terms.reshape(count, -1, terms.shape[1])
    return jnp.sum(lax.all_to_all(blocks, axes, split_axis=0, concat_axis=0), axis=0)


def on_device(
    patches,
    labels,
    op_ids,
    mix_codes,
    aug_gains,
    in_weight,
    dt_weight,
    dt_bias,
    decay_log,
    skip_gain,
    norm_gain,
    out_weight,
    head_weight,
):
    row_count = patches.shape[0]
    ctx_count = lax.axis_size("ctx")
    shards = lax.axis_size("fsdp")
    place = lax.axis_index("fsdp")
    total_patches = row_count * ctx_count * shards
    inner = out_weight.shape[0] * shards
    heads = HEADS // shards
    width = heads * HEAD_DIM
    rows = row_count * shards
    pieces = rows // BLOCK

    patches_all = lax.all_gather(patches, "fsdp", axis=0, tiled=True)
    columns_in = inner + 4 * STATE
    depth = in_weight.shape[0]
    sent_weight = jnp.concatenate(
        [
            in_weight[:, :inner]
            .reshape(depth, heads, shards, HEAD_DIM)
            .transpose(2, 0, 1, 3)
            .reshape(shards, depth, width),
            jnp.broadcast_to(in_weight[None, :, inner:], (shards, depth, 4 * STATE)),
            dt_weight.reshape(depth, 2 * heads, shards).transpose(2, 0, 1),
            jnp.zeros((shards, depth, LANES - 2 * heads), bf16),
        ],
        axis=2,
    )
    mine_weight = lax.all_to_all(sent_weight, "fsdp", split_axis=0, concat_axis=0)
    mine_weight = mine_weight.reshape(D, width + 5 * STATE)
    out_all = lax.all_gather(out_weight, "fsdp", axis=0, tiled=True)
    scales = view_scales(op_ids, mix_codes, aug_gains)
    views = (scales[:, None, :] * patches_all.astype(f32)[None]).astype(bf16)
    projected = dot(views.reshape(VIEWS * rows, D), mine_weight)
    projected = projected.reshape(VIEWS, rows, width + 5 * STATE)
    x = projected[:, :, :width].astype(bf16)
    coef = projected[:, :, width : width + 4 * STATE].astype(bf16)
    raw = projected[:, :, width + 4 * STATE :]

    def local_lanes(values):
        picked = lax.dynamic_index_in_dim(values.reshape(2 * heads, shards), place, 1, False)
        return jnp.pad(picked, (0, LANES - 2 * heads))[None, :]

    bias = local_lanes(dt_bias)
    rate = local_lanes(-jnp.exp(decay_log))
    skip = lax.dynamic_index_in_dim(skip_gain.reshape(heads, shards), place, 1, False)
    skip = jnp.repeat(skip, HEAD_DIM)[None, :]
    gain = norm_gain.reshape(heads, shards, HEAD_DIM)
    gain = lax.dynamic_index_in_dim(gain, place, 1, False).reshape(1, width)

    whole = lambda *dims: pl.BlockSpec((1, *dims), lambda v: (v,) + (0,) * len(dims))
    fixed = lambda *dims: pl.BlockSpec(dims, lambda *_: (0,) * len(dims))
    final, prefix, steps, run, pos = call(
        functools.partial(states_kernel, heads), "states",
        VIEWS * rows * STATE * width * 8, VIEWS * rows * 8192,
        grid=(VIEWS,),
        in_specs=[whole(rows, LANES), whole(rows, width), whole(rows, 4 * STATE),
                  fixed(1, LANES), fixed(1, LANES)],
        out_specs=[whole(2, STATE + LOG_ROWS, width), whole(2, pieces, 2 * STATE, width),
                   whole(rows, LANES), whole(rows, LANES), whole(rows, LANES)],
        out_shape=[
            jax.ShapeDtypeStruct((VIEWS, 2, STATE + LOG_ROWS, width), f32),
            jax.ShapeDtypeStruct((VIEWS, 2, pieces, 2 * STATE, width), bf16),
            jax.ShapeDtypeStruct((VIEWS, rows, LANES), f32),
            jax.ShapeDtypeStruct((VIEWS, rows, LANES), f32),
            jax.ShapeDtypeStruct((VIEWS, rows, LANES), f32),
        ],
    )(raw, x, coef, bias, rate)
    decay = jnp.exp(final[:, :, STATE : STATE + 1, :])
    forward_in = carried_in(final[:, 0, :STATE], decay[:, 0], "ctx", False)
    reverse_in = carried_in(final[:, 1, :STATE], decay[:, 1], "ctx", True)

    local = ()
    for v in range(VIEWS):
        at = lambda *dims, v=v: pl.BlockSpec(
            (1, *dims), lambda i: (v, i) + (0,) * (len(dims) - 1)
        )
        local = (call(
            functools.partial(inside_kernel, heads), "inside",
            rows * D * 8192, rows * 8192,
            grid=(pieces,),
            in_specs=[at(BLOCK, width), at(BLOCK, 4 * STATE),
                      pl.BlockSpec((1, 2, 1, 2 * STATE, width), lambda i, v=v: (v, 0, i, 0, 0)),
                      at(BLOCK, LANES), at(BLOCK, LANES), fixed(1, width)]
            + [pl.BlockSpec(memory_space=pl.ANY)] * len(local),
            out_specs=at(BLOCK, width),
            out_shape=jax.ShapeDtypeStruct((VIEWS, rows, width), f32),
            input_output_aliases={6: 0} if local else {},
        )(x, coef, prefix, steps, run, skip, *local),)
    (local,) = local
    block = lambda *dims: pl.BlockSpec((1, *dims), lambda v, i: (v, i) + (0,) * (len(dims) - 1))
    entering = pl.BlockSpec((1, STATE, width), lambda v, i: (v, 0, 0))

    span = min(rows, 512)
    mixed, squares = call(
        functools.partial(incoming_kernel, heads), "incoming",
        VIEWS * rows * STATE * width * 8, VIEWS * rows * 8192,
        grid=(VIEWS, rows // span),
        in_specs=[
            entering, entering,
            block(span, 4 * STATE), block(span, LANES), block(span, width)],
        out_specs=[block(span, width), pl.BlockSpec((1, 8, span), lambda v, i: (v, 0, i))],
        out_shape=[
            jax.ShapeDtypeStruct((VIEWS, rows, width), f32),
            jax.ShapeDtypeStruct((VIEWS, 8, rows), f32),
        ],
        scratch_shapes=[pltpu.VMEM((2, 2 * STATE, width), bf16)],
    )(forward_in, reverse_in, coef, pos, local)

    square_total = jnp.sum(lax.all_gather(squares[:, 0, :], "fsdp"), axis=0)
    scaling = lax.rsqrt(square_total / inner + 1e-05)
    normed = (mixed * scaling[:, :, None] * gain[None]).astype(bf16)
    outgoing = normed.reshape(VIEWS, shards, row_count, width).transpose(1, 0, 2, 3)
    arrived = lax.all_to_all(outgoing, "fsdp", split_axis=0, concat_axis=0)

    out_own = out_all.reshape(heads, shards, HEAD_DIM, D).transpose(1, 0, 2, 3)
    out_own = out_own.reshape(shards, width, D)
    tile = min(row_count, 128)
    grads, losses, head_term = call(
        functools.partial(tail_kernel, shards, loss_scale / total_patches), "tail",
        VIEWS * row_count * D * 3000, 6 << 20,
        grid=(row_count // tile,),
        in_specs=[
            pl.BlockSpec((shards, VIEWS, tile, width), lambda i: (0, 0, i, 0)),
            fixed(shards, width, D), fixed(D, CLASSES),
            pl.BlockSpec((tile, D), lambda i: (i, 0)),
            fixed(VIEWS, D),
            pl.BlockSpec((tile, 1), lambda i: (i, 0))],
        out_specs=[
            pl.BlockSpec((VIEWS, tile, CLASSES), lambda i: (0, i, 0)),
            pl.BlockSpec((tile, 1), lambda i: (i, 0)),
            fixed(D, CLASSES)],
        out_shape=[
            jax.ShapeDtypeStruct((VIEWS, row_count, CLASSES), bf16),
            jax.ShapeDtypeStruct((row_count, 1), f32),
            jax.ShapeDtypeStruct((D, CLASSES), f32),
        ],
    )(arrived, out_own, head_weight, patches, scales, labels[:, None])

    if ctx_count * shards == HEADS:
        grads_all = lax.all_gather(grads, "fsdp")
        grad_rows = call(
            functools.partial(grad_kernel, shards), "grads",
            VIEWS * rows * D * (width + CLASSES) * 2, 8 << 20,
            grid=(VIEWS, shards),
            in_specs=[
                pl.BlockSpec((1, row_count, width), lambda v, s: (v, s, 0)),
                pl.BlockSpec((1, 1, row_count, CLASSES), lambda v, s: (s, v, 0, 0)),
                fixed(D, CLASSES)],
            out_specs=fixed(width, D),
            out_shape=jax.ShapeDtypeStruct((width, D), f32),
        )(normed, grads_all, head_weight)
        grad_out = scatter_sum(grad_rows, "ctx", ctx_count)
    else:
        grad_hidden = lax.dot_general(
            grads, head_weight, (((2,), (1,)), ((), ())), preferred_element_type=f32
        ).astype(bf16)
        grad_rows = lax.dot_general(
            arrived, grad_hidden, (((1, 2), (0, 1)), ((), ())), preferred_element_type=f32
        )
        grad_rows = grad_rows.reshape(shards, heads, HEAD_DIM, D).transpose(1, 0, 2, 3)
        grad_out = lax.psum_scatter(
            grad_rows.reshape(inner, D), ("ctx", "fsdp"), scatter_dimension=0, tiled=True
        )
    grad_head = scatter_sum(head_term, ("ctx", "fsdp"), ctx_count * shards)
    return (grad_out, grad_head, losses[:, 0])


def solution(mesh):
    return jax.shard_map(
        on_device,
        mesh=mesh,
        in_specs=(
            P(("groups", "ctx", "fsdp"), None),
            P(("groups", "ctx", "fsdp")),
            P("groups", None),
            P("groups", None),
            P(),
            P("fsdp", None),
            P("fsdp", None),
            P(),
            P(),
            P(),
            P(),
            P("fsdp", None),
            P(),
        ),
        out_specs=(
            P(("groups", "ctx", "fsdp"), None),
            P(("groups", "ctx", "fsdp"), None),
            P(("groups", "ctx", "fsdp")),
        ),
        check_vma=False,
    )
```

```python
import functools
import jax
import jax.numpy as jnp
from jax import lax
from jax.experimental import pallas as pl
from jax.experimental.pallas import tpu as pltpu
from jax.sharding import PartitionSpec as P

D = 1024
HEADS = 16
HEAD_DIM = 64
STATE = 128
CLASSES = 128
VIEWS = 3
NOPS = 9
WIDTH_AUG = 3
BLOCK = 128
LANES = 128
LOG_ROWS = 8


loss_scale = 256.0
mix_lambda = 12.0
highest = lax.Precision.HIGHEST
f32 = jnp.float32
bf16 = jnp.bfloat16


def view_scales(op_ids, mix_codes, aug_gains):
    code_values = mix_codes.astype(jnp.float32)
    weights = code_values[:, :WIDTH_AUG] / jnp.sum(
        code_values[:, :WIDTH_AUG], axis=1, keepdims=True
    )
    keep_share = code_values[:, WIDTH_AUG] / 9.0
    onehot = (op_ids[:, :, None] == jnp.arange(NOPS, dtype=jnp.int32)[None, None, :]).astype(
        jnp.float32
    )
    op_weights = jnp.sum(onehot * weights[:, :, None], axis=1)
    mixed_gain = jnp.dot(op_weights, aug_gains, precision=highest)
    scaled = keep_share[:, None] + (1.0 - keep_share[:, None]) * mixed_gain
    return jnp.concatenate([jnp.ones((1, D), jnp.float32), scaled], axis=0)


def halves(value):
    high = value.astype(bf16)
    return high, (value - high.astype(f32)).astype(bf16)


def thirds(value):
    high = value.astype(bf16)
    rest = value - high.astype(f32)
    mid = rest.astype(bf16)
    return high, mid, (rest - mid.astype(f32)).astype(bf16)


def dot(a, b, dims=((1,), (0,))):
    return lax.dot_general(a, b, (dims, ((), ())), preferred_element_type=f32)


def spread(columns, first, heads):
    rows = columns.shape[0]
    lane = lax.broadcasted_iota(jnp.int32, (rows, LANES), 1)
    pieces = []
    for h in range(first, first + heads, 2):
        left = jnp.broadcast_to(columns[:, h : h + 1], (rows, LANES))
        right = jnp.broadcast_to(columns[:, h + 1 : h + 2], (rows, LANES))
        pieces.append(jnp.where(lane < HEAD_DIM, left, right))
    return jnp.concatenate(pieces, axis=1) if len(pieces) > 1 else pieces[0]


def project_kernel(place_ref, patches_ref, scale_ref, weight_ref, x_ref, coef_ref, raw_ref):
    width = x_ref.shape[2]
    patches = patches_ref[...].astype(f32)
    for v in range(VIEWS):
        view = (scale_ref[v : v + 1, :] * patches).astype(bf16)
        out = dot(view, weight_ref[...])
        x_ref[v] = out[:, :width].astype(bf16)
        coef_ref[v] = out[:, width : width + 4 * STATE].astype(bf16)
        raw_ref[v] = out[:, width + 4 * STATE :]


def states_kernel(heads, raw_ref, x_ref, coef_ref, bias_ref, rate_ref,
                  final_ref, prefix_ref, steps_ref, run_ref, pos_ref):
    rows, width = x_ref.shape[1:]
    pieces = rows // BLOCK
    row = lax.broadcasted_iota(jnp.int32, (BLOCK, BLOCK), 0)
    col = lax.broadcasted_iota(jnp.int32, (BLOCK, BLOCK), 1)
    lower = (row >= col).astype(f32).astype(bf16)
    upper = (row <= col).astype(f32).astype(bf16)
    is_forward = col < heads

    def first_pass(i, carried):
        state, total = carried
        at = pl.ds(pl.multiple_of(i * BLOCK, BLOCK), BLOCK)
        raw = raw_ref[0, at, :] + bias_ref[...]
        steps = jnp.maximum(raw, 0.0) + jnp.log1p(jnp.exp(-jnp.abs(raw)))
        parts = thirds(steps * rate_ref[...])
        down = sum(dot(lower, part) for part in parts)
        up = sum(dot(upper, part) for part in parts)
        run = jnp.where(is_forward, down, up)
        steps_ref[0, at, :] = steps
        run_ref[0, at, :] = run
        pos_ref[0, at, :] = run + total
        last = jnp.where(is_forward[:1], run[BLOCK - 1 :], run[:1])
        x = x_ref[0, at, :].astype(f32)
        weight = spread(jnp.exp(last - run) * steps, 0, heads)
        high, low = halves(weight * x)
        write = coef_ref[0, at, :STATE]
        fresh = dot(write, high, ((0,), (0,))) + dot(write, low, ((0,), (0,)))
        s_high, s_low = halves(state)
        prefix_ref[0, 0, i, :STATE, :] = s_high
        prefix_ref[0, 0, i, STATE:, :] = s_low
        return spread(jnp.exp(last), 0, heads) * state + fresh, total + last

    zero = jnp.zeros((STATE, width), f32)
    no_log = jnp.zeros((1, LANES), f32)
    state, total = lax.fori_loop(0, pieces, first_pass, (zero, no_log), unroll=4)
    final_ref[0, 0, :STATE, :] = state
    final_ref[0, 0, STATE:, :] = jnp.broadcast_to(spread(total, 0, heads), (LOG_ROWS, width))

    def second_pass(k, carried):
        state, total = carried
        i = pieces - 1 - k
        at = pl.ds(pl.multiple_of(i * BLOCK, BLOCK), BLOCK)
        run = run_ref[0, at, :]
        last = run[:1]
        pos_ref[0, at, :] = jnp.where(is_forward, pos_ref[0, at, :], run + total)
        x = x_ref[0, at, :].astype(f32)
        weight = spread(jnp.exp(last - run) * steps_ref[0, at, :], heads, heads)
        high, low = halves(weight * x)
        write = coef_ref[0, at, 2 * STATE : 3 * STATE]
        fresh = dot(write, high, ((0,), (0,))) + dot(write, low, ((0,), (0,)))
        s_high, s_low = halves(state)
        prefix_ref[0, 1, i, :STATE, :] = s_high
        prefix_ref[0, 1, i, STATE:, :] = s_low
        return spread(jnp.exp(last), heads, heads) * state + fresh, total + last

    state, total = lax.fori_loop(0, pieces, second_pass, (zero, no_log), unroll=4)
    final_ref[0, 1, :STATE, :] = state
    final_ref[0, 1, STATE:, :] = jnp.broadcast_to(spread(total, heads, heads), (LOG_ROWS, width))


def inside_kernel(heads, x_ref, coef_ref, prefix_ref, steps_ref, run_ref, skip_ref, *rest):
    out_ref = rest[-1]
    row = lax.broadcasted_iota(jnp.int32, (BLOCK, BLOCK), 0)
    col = lax.broadcasted_iota(jnp.int32, (BLOCK, BLOCK), 1)
    below, above = row > col, row < col
    x = x_ref[0]
    steps_t = steps_ref[0].T
    run = run_ref[0]
    run_t = run.T
    coef = coef_ref[0]
    write_f, read_f = coef[:, :STATE], coef[:, STATE : 2 * STATE]
    write_r, read_r = coef[:, 2 * STATE : 3 * STATE], coef[:, 3 * STATE :]
    score_f = dot(read_f, write_f, ((1,), (1,)))
    score_r = dot(read_r, write_r, ((1,), (1,)))
    lane = lax.broadcasted_iota(jnp.int32, (BLOCK, LANES), 1)
    zero = jnp.zeros((BLOCK, LANES), bf16)
    pieces = []
    for pair in range(heads // 2):
        highs, lows = [], []
        for h in (2 * pair, 2 * pair + 1):
            r = heads + h
            gap = jnp.where(
                below, run[:, h : h + 1] - run_t[h : h + 1], run[:, r : r + 1] - run_t[r : r + 1]
            )
            gap = jnp.where(row == col, 0.0, gap)
            from_f = score_f * steps_t[h : h + 1]
            from_r = score_r * steps_t[r : r + 1]
            weight = jnp.where(below, from_f, jnp.where(above, from_r, from_f + from_r))
            high, low = halves(weight * jnp.exp(gap))
            highs.append(high)
            lows.append(low)
        values = x[:, pair * LANES : (pair + 1) * LANES]
        stacked = jnp.concatenate(
            [jnp.where(lane < HEAD_DIM, values, zero), jnp.where(lane < HEAD_DIM, zero, values)],
            axis=0,
        )
        pieces.append(
            dot(jnp.concatenate(highs, axis=1), stacked)
            + dot(jnp.concatenate(lows, axis=1), stacked)
        )
    inside = jnp.concatenate(pieces, axis=1) if len(pieces) > 1 else pieces[0]
    grown = jnp.exp(run)
    carried_f = dot(jnp.concatenate([read_f, read_f], axis=1), prefix_ref[0, 0, 0])
    carried_r = dot(jnp.concatenate([read_r, read_r], axis=1), prefix_ref[0, 1, 0])
    out_ref[0] = (
        inside
        + spread(grown, 0, heads) * carried_f
        + spread(grown, heads, heads) * carried_r
        + skip_ref[...] * x.astype(f32)
    )


def incoming_kernel(heads, forward_ref, reverse_ref, coef_ref, pos_ref, local_ref,
                    mixed_ref, square_ref, held):
    width = local_ref.shape[2]

    @pl.when(pl.program_id(1) == 0)
    def _():
        for way, before in enumerate((forward_ref, reverse_ref)):
            high, low = halves(before[0])
            held[way, :STATE, :] = high
            held[way, STATE:, :] = low

    grown = jnp.exp(pos_ref[0])
    coef = coef_ref[0]
    read_f = coef[:, STATE : 2 * STATE]
    read_r = coef[:, 3 * STATE :]
    mixed = (
        local_ref[0]
        + spread(grown, 0, heads) * dot(jnp.concatenate([read_f, read_f], axis=1), held[0])
        + spread(grown, heads, heads) * dot(jnp.concatenate([read_r, read_r], axis=1), held[1])
    )
    mixed_ref[0] = mixed
    ones = jnp.ones((8, width), bf16)
    square_ref[0] = sum(dot(ones, part, ((1,), (1,))) for part in thirds(mixed * mixed))


def tail_kernel(shards, factor, normed_ref, out_w_ref, head_ref, patches_ref, scale_ref,
                label_ref, logit_ref, loss_ref, head_grad_ref, hidden_ref=None):
    rows = patches_ref.shape[0]
    head = head_ref[...]
    patches = patches_ref[...].astype(f32)
    hiddens, logs = [], []
    for v in range(VIEWS):
        total = dot(normed_ref[0, v], out_w_ref[0])
        for s in range(1, shards):
            total += dot(normed_ref[s, v], out_w_ref[s])
        view = (scale_ref[v : v + 1, :] * patches).astype(bf16)
        hidden = (view.astype(f32) + total).astype(bf16)
        hiddens.append(hidden)
        logits = dot(hidden, head)
        shifted = logits - jnp.max(logits, axis=1, keepdims=True)
        logs.append(shifted - jnp.log(jnp.sum(jnp.exp(shifted), axis=1, keepdims=True)))
    top = jnp.maximum(jnp.maximum(logs[0], logs[1]), logs[2])
    mean = top + jnp.log(sum(jnp.exp(log - top) for log in logs)) - jnp.log(f32(VIEWS))
    lane = lax.broadcasted_iota(jnp.int32, (rows, CLASSES), 1)
    onehot = (lane == label_ref[...]).astype(f32)
    spread_sum = jnp.zeros((rows, 1), f32)
    grads = []
    for v in range(VIEWS):
        prob = jnp.exp(logs[v])
        gap = logs[v] - mean
        inner = jnp.sum(prob * gap, axis=1, keepdims=True)
        spread_sum += inner
        grad = (mix_lambda / VIEWS) * prob * (gap - inner)
        if v == 0:
            grad += prob - onehot
        grads.append((factor * grad).astype(bf16))
        logit_ref[v] = grads[v]
    cross = -jnp.sum(onehot * logs[0], axis=1, keepdims=True)
    loss_ref[...] = cross + mix_lambda * (spread_sum / VIEWS)
    update = sum(dot(hiddens[v], grads[v], ((0,), (0,))) for v in range(VIEWS))

    @pl.when(pl.program_id(0) == 0)
    def _():
        head_grad_ref[...] = update

    @pl.when(pl.program_id(0) > 0)
    def _():
        head_grad_ref[...] += update


def grad_kernel(shards, normed_ref, logit_ref, head_ref, out_ref):
    grads = logit_ref[0, 0]
    hidden = dot(grads, head_ref[...], ((1,), (1,))).astype(bf16)
    update = dot(normed_ref[0], hidden, ((0,), (0,)))
    first = (pl.program_id(0) == 0) & (pl.program_id(1) == 0)

    @pl.when(first)
    def _():
        out_ref[...] = update

    @pl.when(jnp.logical_not(first))
    def _():
        out_ref[...] += update


def call(kernel, name, flops, moved, limit=48 << 20, **options):
    return pl.pallas_call(
        kernel,
        name=name,
        compiler_params=pltpu.CompilerParams(vmem_limit_bytes=limit),
        cost_estimate=pl.CostEstimate(flops=flops, bytes_accessed=moved, transcendentals=0),
        **options,
    )


def carried_in(state, decay, axis, reverse):
    count = lax.axis_size(axis)
    if reverse:
        hops = [(j, j - 1) for j in range(1, count)]
    else:
        hops = [(j, j + 1) for j in range(count - 1)]
    sent, got = state, jnp.zeros_like(state)
    for hop in range(count - 1):
        got = lax.ppermute(sent, axis, hops)
        sent = decay * got + state
    return got


def scatter_sum(terms, axes, count):
    blocks = terms.reshape(count, -1, terms.shape[1])
    return jnp.sum(lax.all_to_all(blocks, axes, split_axis=0, concat_axis=0), axis=0)


def on_device(
    patches,
    labels,
    op_ids,
    mix_codes,
    aug_gains,
    in_weight,
    dt_weight,
    dt_bias,
    decay_log,
    skip_gain,
    norm_gain,
    out_weight,
    head_weight,
):
    row_count = patches.shape[0]
    ctx_count = lax.axis_size("ctx")
    shards = lax.axis_size("fsdp")
    place = lax.axis_index("fsdp")
    total_patches = row_count * ctx_count * shards
    inner = out_weight.shape[0] * shards
    heads = HEADS // shards
    width = heads * HEAD_DIM
    rows = row_count * shards
    pieces = rows // BLOCK

    if shards == 4:
        across = lax.ppermute(patches, "fsdp", [(f, f ^ 2) for f in range(shards)])
        beside = lax.ppermute(patches, "fsdp", [(f, f ^ 1) for f in range(shards)])
        corner = lax.ppermute(across, "fsdp", [(f, f ^ 1) for f in range(shards)])
        patches_all = jnp.concatenate([patches, beside, across, corner], axis=0)
        flip = place
    else:
        patches_all = lax.all_gather(patches, "fsdp", axis=0, tiled=True)
        flip = jnp.zeros_like(place)
    columns_in = inner + 4 * STATE
    depth = in_weight.shape[0]
    sent_weight = jnp.concatenate(
        [
            in_weight[:, :inner]
            .reshape(depth, heads, shards, HEAD_DIM)
            .transpose(2, 0, 1, 3)
            .reshape(shards, depth, width),
            jnp.broadcast_to(in_weight[None, :, inner:], (shards, depth, 4 * STATE)),
            dt_weight.reshape(depth, 2 * heads, shards).transpose(2, 0, 1),
            jnp.zeros((shards, depth, LANES - 2 * heads), bf16),
        ],
        axis=2,
    )
    mine_weight = lax.all_to_all(sent_weight, "fsdp", split_axis=0, concat_axis=0)
    mine_weight = mine_weight.reshape(D, width + 5 * STATE)
    scales = view_scales(op_ids, mix_codes, aug_gains)
    tile = min(row_count, 128)
    per = row_count // tile
    placed = lambda s, i, flip_ref: ((s ^ flip_ref[0]) * per + i, 0)
    piece = lambda lanes: pl.BlockSpec((VIEWS, tile, lanes), lambda s, i, _: (0, s * per + i, 0))
    constant = lambda *dims: pl.BlockSpec(dims, lambda *_: (0,) * len(dims))
    x, coef, raw = call(
        project_kernel, "project",
        VIEWS * rows * D * (width + 5 * STATE) * 2, rows * D * 8,
        grid_spec=pltpu.PrefetchScalarGridSpec(
            num_scalar_prefetch=1,
            grid=(shards, per),
            in_specs=[pl.BlockSpec((tile, D), placed), constant(VIEWS, D),
                      constant(D, width + 5 * STATE)],
            out_specs=[piece(width), piece(4 * STATE), piece(LANES)],
        ),
        out_shape=[
            jax.ShapeDtypeStruct((VIEWS, rows, width), bf16),
            jax.ShapeDtypeStruct((VIEWS, rows, 4 * STATE), bf16),
            jax.ShapeDtypeStruct((VIEWS, rows, LANES), f32),
        ],
    )(flip.reshape(1).astype(jnp.int32), patches_all, scales, mine_weight)
    raw, out_later = lax.optimization_barrier((raw, out_weight))
    out_all = lax.all_gather(out_later, "fsdp", axis=0, tiled=True)

    def local_lanes(values):
        picked = lax.dynamic_index_in_dim(values.reshape(2 * heads, shards), place, 1, False)
        return jnp.pad(picked, (0, LANES - 2 * heads))[None, :]

    bias = local_lanes(dt_bias)
    rate = local_lanes(-jnp.exp(decay_log))
    skip = lax.dynamic_index_in_dim(skip_gain.reshape(heads, shards), place, 1, False)
    skip = jnp.repeat(skip, HEAD_DIM)[None, :]
    gain = norm_gain.reshape(heads, shards, HEAD_DIM)
    gain = lax.dynamic_index_in_dim(gain, place, 1, False).reshape(1, width)

    whole = lambda *dims: pl.BlockSpec((1, *dims), lambda v: (v,) + (0,) * len(dims))
    fixed = lambda *dims: pl.BlockSpec(dims, lambda *_: (0,) * len(dims))
    final, prefix, steps, run, pos = call(
        functools.partial(states_kernel, heads), "states",
        VIEWS * rows * STATE * width * 8, VIEWS * rows * 8192,
        grid=(VIEWS,),
        in_specs=[whole(rows, LANES), whole(rows, width), whole(rows, 4 * STATE),
                  fixed(1, LANES), fixed(1, LANES)],
        out_specs=[whole(2, STATE + LOG_ROWS, width), whole(2, pieces, 2 * STATE, width),
                   whole(rows, LANES), whole(rows, LANES), whole(rows, LANES)],
        out_shape=[
            jax.ShapeDtypeStruct((VIEWS, 2, STATE + LOG_ROWS, width), f32),
            jax.ShapeDtypeStruct((VIEWS, 2, pieces, 2 * STATE, width), bf16),
            jax.ShapeDtypeStruct((VIEWS, rows, LANES), f32),
            jax.ShapeDtypeStruct((VIEWS, rows, LANES), f32),
            jax.ShapeDtypeStruct((VIEWS, rows, LANES), f32),
        ],
    )(raw, x, coef, bias, rate)
    decay = jnp.exp(final[:, :, STATE : STATE + 1, :])
    forward_in = carried_in(final[:, 0, :STATE], decay[:, 0], "ctx", False)
    reverse_in = carried_in(final[:, 1, :STATE], decay[:, 1], "ctx", True)

    local = ()
    for v in range(VIEWS):
        at = lambda *dims, v=v: pl.BlockSpec(
            (1, *dims), lambda i: (v, i) + (0,) * (len(dims) - 1)
        )
        local = (call(
            functools.partial(inside_kernel, heads), "inside",
            rows * D * 8192, rows * 8192,
            grid=(pieces,),
            in_specs=[at(BLOCK, width), at(BLOCK, 4 * STATE),
                      pl.BlockSpec((1, 2, 1, 2 * STATE, width), lambda i, v=v: (v, 0, i, 0, 0)),
                      at(BLOCK, LANES), at(BLOCK, LANES), fixed(1, width)]
            + [pl.BlockSpec(memory_space=pl.ANY)] * len(local),
            out_specs=at(BLOCK, width),
            out_shape=jax.ShapeDtypeStruct((VIEWS, rows, width), f32),
            input_output_aliases={6: 0} if local else {},
        )(x, coef, prefix, steps, run, skip, *local),)
    (local,) = local
    block = lambda *dims: pl.BlockSpec((1, *dims), lambda v, i: (v, i) + (0,) * (len(dims) - 1))
    entering = pl.BlockSpec((1, STATE, width), lambda v, i: (v, 0, 0))

    span = min(rows, 512)
    mixed, squares = call(
        functools.partial(incoming_kernel, heads), "incoming",
        VIEWS * rows * STATE * width * 8, VIEWS * rows * 8192,
        grid=(VIEWS, rows // span),
        in_specs=[
            entering, entering,
            block(span, 4 * STATE), block(span, LANES), block(span, width)],
        out_specs=[block(span, width), pl.BlockSpec((1, 8, span), lambda v, i: (v, 0, i))],
        out_shape=[
            jax.ShapeDtypeStruct((VIEWS, rows, width), f32),
            jax.ShapeDtypeStruct((VIEWS, 8, rows), f32),
        ],
        scratch_shapes=[pltpu.VMEM((2, 2 * STATE, width), bf16)],
    )(forward_in, reverse_in, coef, pos, local)

    square_total = jnp.sum(lax.all_gather(squares[:, 0, :], "fsdp"), axis=0)
    scaling = lax.rsqrt(square_total / inner + 1e-05)
    normed = (mixed * scaling[:, :, None] * gain[None]).astype(bf16)
    outgoing = normed.reshape(VIEWS, shards, row_count, width).transpose(1, 0, 2, 3)
    arrived = lax.all_to_all(outgoing, "fsdp", split_axis=0, concat_axis=0)

    out_own = out_all.reshape(heads, shards, HEAD_DIM, D).transpose(1, 0, 2, 3)
    out_own = out_own.reshape(shards, width, D)
    tile = min(row_count, 128)
    grads, losses, head_term = call(
        functools.partial(tail_kernel, shards, loss_scale / total_patches), "tail",
        VIEWS * row_count * D * 3000, 6 << 20,
        grid=(row_count // tile,),
        in_specs=[
            pl.BlockSpec((shards, VIEWS, tile, width), lambda i: (0, 0, i, 0)),
            fixed(shards, width, D), fixed(D, CLASSES),
            pl.BlockSpec((tile, D), lambda i: (i, 0)),
            fixed(VIEWS, D),
            pl.BlockSpec((tile, 1), lambda i: (i, 0))],
        out_specs=[
            pl.BlockSpec((VIEWS, tile, CLASSES), lambda i: (0, i, 0)),
            pl.BlockSpec((tile, 1), lambda i: (i, 0)),
            fixed(D, CLASSES)],
        out_shape=[
            jax.ShapeDtypeStruct((VIEWS, row_count, CLASSES), bf16),
            jax.ShapeDtypeStruct((row_count, 1), f32),
            jax.ShapeDtypeStruct((D, CLASSES), f32),
        ],
    )(arrived, out_own, head_weight, patches, scales, labels[:, None])

    if ctx_count * shards == HEADS:
        grads_all = lax.all_gather(grads, "fsdp")
        grads_all, head_term = lax.optimization_barrier((grads_all, head_term))
        half = D // 2
        sums = []
        for k in range(2):
            grad_rows = call(
                functools.partial(grad_kernel, shards), "grads",
                VIEWS * rows * D * (width + CLASSES) * 4, 8 << 20,
                grid=(VIEWS, shards),
                in_specs=[
                    pl.BlockSpec((1, row_count, width), lambda v, s: (v, s, 0)),
                    pl.BlockSpec((1, 1, row_count, CLASSES), lambda v, s: (s, v, 0, 0)),
                    pl.BlockSpec((half, CLASSES), lambda v, s, k=k: (k, 0))],
                out_specs=fixed(width, half),
                out_shape=jax.ShapeDtypeStruct((width, half), f32),
            )(normed, grads_all, head_weight)
            sums.append(scatter_sum(grad_rows, "ctx", ctx_count))
        grad_out = jnp.concatenate(sums, axis=1)
    else:
        grad_hidden = lax.dot_general(
            grads, head_weight, (((2,), (1,)), ((), ())), preferred_element_type=f32
        ).astype(bf16)
        grad_rows = lax.dot_general(
            arrived, grad_hidden, (((1, 2), (0, 1)), ((), ())), preferred_element_type=f32
        )
        grad_rows = grad_rows.reshape(shards, heads, HEAD_DIM, D).transpose(1, 0, 2, 3)
        grad_out = lax.psum_scatter(
            grad_rows.reshape(inner, D), ("ctx", "fsdp"), scatter_dimension=0, tiled=True
        )
    grad_head = scatter_sum(head_term, ("ctx", "fsdp"), ctx_count * shards)
    return (grad_out, grad_head, losses[:, 0])


def solution(mesh):
    return jax.shard_map(
        on_device,
        mesh=mesh,
        in_specs=(
            P(("groups", "ctx", "fsdp"), None),
            P(("groups", "ctx", "fsdp")),
            P("groups", None),
            P("groups", None),
            P(),
            P("fsdp", None),
            P("fsdp", None),
            P(),
            P(),
            P(),
            P(),
            P("fsdp", None),
            P(),
        ),
        out_specs=(
            P(("groups", "ctx", "fsdp"), None),
            P(("groups", "ctx", "fsdp"), None),
            P(("groups", "ctx", "fsdp")),
        ),
        check_vma=False,
    )
```

```python
import functools
import jax
import jax.numpy as jnp
from jax import lax
from jax.experimental import pallas as pl
from jax.experimental.pallas import tpu as pltpu
from jax.sharding import PartitionSpec as P

D = 1024
HEADS = 16
HEAD_DIM = 64
STATE = 128
CLASSES = 128
VIEWS = 3
NOPS = 9
WIDTH_AUG = 3
BLOCK = 128
LANES = 128
LOG_ROWS = 8


loss_scale = 256.0
mix_lambda = 12.0
highest = lax.Precision.HIGHEST
f32 = jnp.float32
bf16 = jnp.bfloat16


def view_scales(op_ids, mix_codes, aug_gains):
    code_values = mix_codes.astype(jnp.float32)
    weights = code_values[:, :WIDTH_AUG] / jnp.sum(
        code_values[:, :WIDTH_AUG], axis=1, keepdims=True
    )
    keep_share = code_values[:, WIDTH_AUG] / 9.0
    onehot = (op_ids[:, :, None] == jnp.arange(NOPS, dtype=jnp.int32)[None, None, :]).astype(
        jnp.float32
    )
    op_weights = jnp.sum(onehot * weights[:, :, None], axis=1)
    mixed_gain = jnp.dot(op_weights, aug_gains, precision=highest)
    scaled = keep_share[:, None] + (1.0 - keep_share[:, None]) * mixed_gain
    return jnp.concatenate([jnp.ones((1, D), jnp.float32), scaled], axis=0)


def halves(value):
    high = value.astype(bf16)
    return high, (value - high.astype(f32)).astype(bf16)


def thirds(value):
    high = value.astype(bf16)
    rest = value - high.astype(f32)
    mid = rest.astype(bf16)
    return high, mid, (rest - mid.astype(f32)).astype(bf16)


def dot(a, b, dims=((1,), (0,))):
    return lax.dot_general(a, b, (dims, ((), ())), preferred_element_type=f32)


def spread(columns, first, heads):
    rows = columns.shape[0]
    lane = lax.broadcasted_iota(jnp.int32, (rows, LANES), 1)
    pieces = []
    for h in range(first, first + heads, 2):
        left = jnp.broadcast_to(columns[:, h : h + 1], (rows, LANES))
        right = jnp.broadcast_to(columns[:, h + 1 : h + 2], (rows, LANES))
        pieces.append(jnp.where(lane < HEAD_DIM, left, right))
    return jnp.concatenate(pieces, axis=1) if len(pieces) > 1 else pieces[0]


def project_kernel(place_ref, patches_ref, scale_ref, weight_ref, x_ref, coef_ref, raw_ref):
    width = x_ref.shape[2]
    patches = patches_ref[...].astype(f32)
    for v in range(VIEWS):
        view = (scale_ref[v : v + 1, :] * patches).astype(bf16)
        out = dot(view, weight_ref[...])
        x_ref[v] = out[:, :width].astype(bf16)
        coef_ref[v] = out[:, width : width + 4 * STATE].astype(bf16)
        raw_ref[v] = out[:, width + 4 * STATE :]


def states_kernel(heads, raw_ref, x_ref, coef_ref, bias_ref, rate_ref,
                  final_ref, prefix_ref, steps_ref, run_ref, pos_ref):
    rows, width = x_ref.shape[1:]
    pieces = rows // BLOCK
    row = lax.broadcasted_iota(jnp.int32, (BLOCK, BLOCK), 0)
    col = lax.broadcasted_iota(jnp.int32, (BLOCK, BLOCK), 1)
    lower = (row >= col).astype(f32).astype(bf16)
    upper = (row <= col).astype(f32).astype(bf16)
    is_forward = col < heads

    def first_pass(i, carried):
        state, total = carried
        at = pl.ds(pl.multiple_of(i * BLOCK, BLOCK), BLOCK)
        raw = raw_ref[0, at, :] + bias_ref[...]
        steps = jnp.maximum(raw, 0.0) + jnp.log1p(jnp.exp(-jnp.abs(raw)))
        parts = thirds(steps * rate_ref[...])
        down = sum(dot(lower, part) for part in parts)
        up = sum(dot(upper, part) for part in parts)
        run = jnp.where(is_forward, down, up)
        steps_ref[0, at, :] = steps
        run_ref[0, at, :] = run
        pos_ref[0, at, :] = run + total
        last = jnp.where(is_forward[:1], run[BLOCK - 1 :], run[:1])
        x = x_ref[0, at, :].astype(f32)
        weight = spread(jnp.exp(last - run) * steps, 0, heads)
        high, low = halves(weight * x)
        write = coef_ref[0, at, :STATE]
        fresh = dot(write, high, ((0,), (0,))) + dot(write, low, ((0,), (0,)))
        s_high, s_low = halves(state)
        prefix_ref[0, 0, i, :STATE, :] = s_high
        prefix_ref[0, 0, i, STATE:, :] = s_low
        return spread(jnp.exp(last), 0, heads) * state + fresh, total + last

    zero = jnp.zeros((STATE, width), f32)
    no_log = jnp.zeros((1, LANES), f32)
    state, total = lax.fori_loop(0, pieces, first_pass, (zero, no_log), unroll=4)
    final_ref[0, 0, :STATE, :] = state
    final_ref[0, 0, STATE:, :] = jnp.broadcast_to(spread(total, 0, heads), (LOG_ROWS, width))

    def second_pass(k, carried):
        state, total = carried
        i = pieces - 1 - k
        at = pl.ds(pl.multiple_of(i * BLOCK, BLOCK), BLOCK)
        run = run_ref[0, at, :]
        last = run[:1]
        pos_ref[0, at, :] = jnp.where(is_forward, pos_ref[0, at, :], run + total)
        x = x_ref[0, at, :].astype(f32)
        weight = spread(jnp.exp(last - run) * steps_ref[0, at, :], heads, heads)
        high, low = halves(weight * x)
        write = coef_ref[0, at, 2 * STATE : 3 * STATE]
        fresh = dot(write, high, ((0,), (0,))) + dot(write, low, ((0,), (0,)))
        s_high, s_low = halves(state)
        prefix_ref[0, 1, i, :STATE, :] = s_high
        prefix_ref[0, 1, i, STATE:, :] = s_low
        return spread(jnp.exp(last), heads, heads) * state + fresh, total + last

    state, total = lax.fori_loop(0, pieces, second_pass, (zero, no_log), unroll=4)
    final_ref[0, 1, :STATE, :] = state
    final_ref[0, 1, STATE:, :] = jnp.broadcast_to(spread(total, heads, heads), (LOG_ROWS, width))


def inside_kernel(heads, x_ref, coef_ref, prefix_ref, steps_ref, run_ref, skip_ref, *rest):
    out_ref = rest[-1]
    row = lax.broadcasted_iota(jnp.int32, (BLOCK, BLOCK), 0)
    col = lax.broadcasted_iota(jnp.int32, (BLOCK, BLOCK), 1)
    below, above = row > col, row < col
    x = x_ref[0]
    steps_t = steps_ref[0].T
    run = run_ref[0]
    run_t = run.T
    coef = coef_ref[0]
    write_f, read_f = coef[:, :STATE], coef[:, STATE : 2 * STATE]
    write_r, read_r = coef[:, 2 * STATE : 3 * STATE], coef[:, 3 * STATE :]
    score_f = dot(read_f, write_f, ((1,), (1,)))
    score_r = dot(read_r, write_r, ((1,), (1,)))
    lane = lax.broadcasted_iota(jnp.int32, (BLOCK, LANES), 1)
    zero = jnp.zeros((BLOCK, LANES), bf16)
    pieces = []
    for pair in range(heads // 2):
        highs, lows = [], []
        for h in (2 * pair, 2 * pair + 1):
            r = heads + h
            gap = jnp.where(
                below, run[:, h : h + 1] - run_t[h : h + 1], run[:, r : r + 1] - run_t[r : r + 1]
            )
            gap = jnp.where(row == col, 0.0, gap)
            from_f = score_f * steps_t[h : h + 1]
            from_r = score_r * steps_t[r : r + 1]
            weight = jnp.where(below, from_f, jnp.where(above, from_r, from_f + from_r))
            high, low = halves(weight * jnp.exp(gap))
            highs.append(high)
            lows.append(low)
        values = x[:, pair * LANES : (pair + 1) * LANES]
        stacked = jnp.concatenate(
            [jnp.where(lane < HEAD_DIM, values, zero), jnp.where(lane < HEAD_DIM, zero, values)],
            axis=0,
        )
        pieces.append(
            dot(jnp.concatenate(highs, axis=1), stacked)
            + dot(jnp.concatenate(lows, axis=1), stacked)
        )
    inside = jnp.concatenate(pieces, axis=1) if len(pieces) > 1 else pieces[0]
    grown = jnp.exp(run)
    carried_f = dot(jnp.concatenate([read_f, read_f], axis=1), prefix_ref[0, 0, 0])
    carried_r = dot(jnp.concatenate([read_r, read_r], axis=1), prefix_ref[0, 1, 0])
    out_ref[0] = (
        inside
        + spread(grown, 0, heads) * carried_f
        + spread(grown, heads, heads) * carried_r
        + skip_ref[...] * x.astype(f32)
    )


def incoming_kernel(heads, forward_ref, reverse_ref, coef_ref, pos_ref, local_ref,
                    mixed_ref, square_ref, held):
    width = local_ref.shape[2]

    @pl.when(pl.program_id(1) == 0)
    def _():
        for way, before in enumerate((forward_ref, reverse_ref)):
            high, low = halves(before[0])
            held[way, :STATE, :] = high
            held[way, STATE:, :] = low

    grown = jnp.exp(pos_ref[0])
    coef = coef_ref[0]
    read_f = coef[:, STATE : 2 * STATE]
    read_r = coef[:, 3 * STATE :]
    mixed = (
        local_ref[0]
        + spread(grown, 0, heads) * dot(jnp.concatenate([read_f, read_f], axis=1), held[0])
        + spread(grown, heads, heads) * dot(jnp.concatenate([read_r, read_r], axis=1), held[1])
    )
    mixed_ref[0] = mixed
    ones = jnp.ones((8, width), bf16)
    square_ref[0] = sum(dot(ones, part, ((1,), (1,))) for part in thirds(mixed * mixed))


def tail_kernel(shards, factor, normed_ref, out_w_ref, head_ref, patches_ref, scale_ref,
                label_ref, logit_ref, loss_ref, head_grad_ref, hidden_ref=None):
    rows = patches_ref.shape[0]
    head = head_ref[...]
    patches = patches_ref[...].astype(f32)
    hiddens, logs = [], []
    for v in range(VIEWS):
        total = dot(normed_ref[0, v], out_w_ref[0])
        for s in range(1, shards):
            total += dot(normed_ref[s, v], out_w_ref[s])
        view = (scale_ref[v : v + 1, :] * patches).astype(bf16)
        hidden = (view.astype(f32) + total).astype(bf16)
        hiddens.append(hidden)
        logits = dot(hidden, head)
        shifted = logits - jnp.max(logits, axis=1, keepdims=True)
        logs.append(shifted - jnp.log(jnp.sum(jnp.exp(shifted), axis=1, keepdims=True)))
    top = jnp.maximum(jnp.maximum(logs[0], logs[1]), logs[2])
    mean = top + jnp.log(sum(jnp.exp(log - top) for log in logs)) - jnp.log(f32(VIEWS))
    lane = lax.broadcasted_iota(jnp.int32, (rows, CLASSES), 1)
    onehot = (lane == label_ref[...]).astype(f32)
    spread_sum = jnp.zeros((rows, 1), f32)
    grads = []
    for v in range(VIEWS):
        prob = jnp.exp(logs[v])
        gap = logs[v] - mean
        inner = jnp.sum(prob * gap, axis=1, keepdims=True)
        spread_sum += inner
        grad = (mix_lambda / VIEWS) * prob * (gap - inner)
        if v == 0:
            grad += prob - onehot
        grads.append((factor * grad).astype(bf16))
        logit_ref[v] = grads[v]
    cross = -jnp.sum(onehot * logs[0], axis=1, keepdims=True)
    loss_ref[...] = cross + mix_lambda * (spread_sum / VIEWS)
    update = sum(dot(hiddens[v], grads[v], ((0,), (0,))) for v in range(VIEWS))

    @pl.when(pl.program_id(0) == 0)
    def _():
        head_grad_ref[...] = update

    @pl.when(pl.program_id(0) > 0)
    def _():
        head_grad_ref[...] += update


def grad_kernel(shards, normed_ref, logit_ref, head_ref, out_ref):
    grads = logit_ref[0, 0]
    hidden = dot(grads, head_ref[...], ((1,), (1,))).astype(bf16)
    update = dot(normed_ref[0], hidden, ((0,), (0,)))
    first = (pl.program_id(0) == 0) & (pl.program_id(1) == 0)

    @pl.when(first)
    def _():
        out_ref[...] = update

    @pl.when(jnp.logical_not(first))
    def _():
        out_ref[...] += update


def call(kernel, name, flops, moved, limit=48 << 20, **options):
    return pl.pallas_call(
        kernel,
        name=name,
        compiler_params=pltpu.CompilerParams(vmem_limit_bytes=limit),
        cost_estimate=pl.CostEstimate(flops=flops, bytes_accessed=moved, transcendentals=0),
        **options,
    )


def carried_in(state, decay, axis, reverse):
    count = lax.axis_size(axis)
    if reverse:
        hops = [(j, j - 1) for j in range(1, count)]
    else:
        hops = [(j, j + 1) for j in range(count - 1)]
    sent, got = state, jnp.zeros_like(state)
    for hop in range(count - 1):
        got = lax.ppermute(sent, axis, hops)
        sent = decay * got + state
    return got


def scatter_sum(terms, axes, count):
    blocks = terms.reshape(count, -1, terms.shape[1])
    return jnp.sum(lax.all_to_all(blocks, axes, split_axis=0, concat_axis=0), axis=0)


def on_device(
    patches,
    labels,
    op_ids,
    mix_codes,
    aug_gains,
    in_weight,
    dt_weight,
    dt_bias,
    decay_log,
    skip_gain,
    norm_gain,
    out_weight,
    head_weight,
):
    row_count = patches.shape[0]
    ctx_count = lax.axis_size("ctx")
    shards = lax.axis_size("fsdp")
    place = lax.axis_index("fsdp")
    total_patches = row_count * ctx_count * shards
    inner = out_weight.shape[0] * shards
    heads = HEADS // shards
    width = heads * HEAD_DIM
    rows = row_count * shards
    pieces = rows // BLOCK

    if shards == 4:
        across = lax.ppermute(patches, "fsdp", [(f, f ^ 2) for f in range(shards)])
        beside = lax.ppermute(patches, "fsdp", [(f, f ^ 1) for f in range(shards)])
        corner = lax.ppermute(across, "fsdp", [(f, f ^ 1) for f in range(shards)])
        patches_all = jnp.concatenate([patches, beside, across, corner], axis=0)
        flip = place
    else:
        patches_all = lax.all_gather(patches, "fsdp", axis=0, tiled=True)
        flip = jnp.zeros_like(place)
    columns_in = inner + 4 * STATE
    depth = in_weight.shape[0]
    sent_weight = jnp.concatenate(
        [
            in_weight[:, :inner]
            .reshape(depth, heads, shards, HEAD_DIM)
            .transpose(2, 0, 1, 3)
            .reshape(shards, depth, width),
            jnp.broadcast_to(in_weight[None, :, inner:], (shards, depth, 4 * STATE)),
            dt_weight.reshape(depth, 2 * heads, shards).transpose(2, 0, 1),
            jnp.zeros((shards, depth, LANES - 2 * heads), bf16),
        ],
        axis=2,
    )
    mine_weight = lax.all_to_all(sent_weight, "fsdp", split_axis=0, concat_axis=0)
    mine_weight = mine_weight.reshape(D, width + 5 * STATE)
    scales = view_scales(op_ids, mix_codes, aug_gains)
    tile = min(row_count, 128)
    per = row_count // tile
    placed = lambda s, i, flip_ref: ((s ^ flip_ref[0]) * per + i, 0)
    piece = lambda lanes: pl.BlockSpec((VIEWS, tile, lanes), lambda s, i, _: (0, s * per + i, 0))
    constant = lambda *dims: pl.BlockSpec(dims, lambda *_: (0,) * len(dims))
    x, coef, raw = call(
        project_kernel, "project",
        VIEWS * rows * D * (width + 5 * STATE) * 2, rows * D * 8,
        grid_spec=pltpu.PrefetchScalarGridSpec(
            num_scalar_prefetch=1,
            grid=(shards, per),
            in_specs=[pl.BlockSpec((tile, D), placed), constant(VIEWS, D),
                      constant(D, width + 5 * STATE)],
            out_specs=[piece(width), piece(4 * STATE), piece(LANES)],
        ),
        out_shape=[
            jax.ShapeDtypeStruct((VIEWS, rows, width), bf16),
            jax.ShapeDtypeStruct((VIEWS, rows, 4 * STATE), bf16),
            jax.ShapeDtypeStruct((VIEWS, rows, LANES), f32),
        ],
    )(flip.reshape(1).astype(jnp.int32), patches_all, scales, mine_weight)
    raw, out_later = lax.optimization_barrier((raw, out_weight))
    out_all = lax.all_gather(out_later, "fsdp", axis=0, tiled=True)

    def local_lanes(values):
        picked = lax.dynamic_index_in_dim(values.reshape(2 * heads, shards), place, 1, False)
        return jnp.pad(picked, (0, LANES - 2 * heads))[None, :]

    bias = local_lanes(dt_bias)
    rate = local_lanes(-jnp.exp(decay_log))
    skip = lax.dynamic_index_in_dim(skip_gain.reshape(heads, shards), place, 1, False)
    skip = jnp.repeat(skip, HEAD_DIM)[None, :]
    gain = norm_gain.reshape(heads, shards, HEAD_DIM)
    gain = lax.dynamic_index_in_dim(gain, place, 1, False).reshape(1, width)

    whole = lambda *dims: pl.BlockSpec((1, *dims), lambda v: (v,) + (0,) * len(dims))
    fixed = lambda *dims: pl.BlockSpec(dims, lambda *_: (0,) * len(dims))
    final, prefix, steps, run, pos = call(
        functools.partial(states_kernel, heads), "states",
        VIEWS * rows * STATE * width * 8, VIEWS * rows * 8192,
        grid=(VIEWS,),
        in_specs=[whole(rows, LANES), whole(rows, width), whole(rows, 4 * STATE),
                  fixed(1, LANES), fixed(1, LANES)],
        out_specs=[whole(2, STATE + LOG_ROWS, width), whole(2, pieces, 2 * STATE, width),
                   whole(rows, LANES), whole(rows, LANES), whole(rows, LANES)],
        out_shape=[
            jax.ShapeDtypeStruct((VIEWS, 2, STATE + LOG_ROWS, width), f32),
            jax.ShapeDtypeStruct((VIEWS, 2, pieces, 2 * STATE, width), bf16),
            jax.ShapeDtypeStruct((VIEWS, rows, LANES), f32),
            jax.ShapeDtypeStruct((VIEWS, rows, LANES), f32),
            jax.ShapeDtypeStruct((VIEWS, rows, LANES), f32),
        ],
    )(raw, x, coef, bias, rate)
    decay = jnp.exp(final[:, :, STATE : STATE + 1, :])
    forward_in = carried_in(final[:, 0, :STATE], decay[:, 0], "ctx", False)
    reverse_in = carried_in(final[:, 1, :STATE], decay[:, 1], "ctx", True)

    local = ()
    for v in range(VIEWS):
        at = lambda *dims, v=v: pl.BlockSpec(
            (1, *dims), lambda i: (v, i) + (0,) * (len(dims) - 1)
        )
        local = (call(
            functools.partial(inside_kernel, heads), "inside",
            rows * D * 8192, rows * 8192,
            grid=(pieces,),
            in_specs=[at(BLOCK, width), at(BLOCK, 4 * STATE),
                      pl.BlockSpec((1, 2, 1, 2 * STATE, width), lambda i, v=v: (v, 0, i, 0, 0)),
                      at(BLOCK, LANES), at(BLOCK, LANES), fixed(1, width)]
            + [pl.BlockSpec(memory_space=pl.ANY)] * len(local),
            out_specs=at(BLOCK, width),
            out_shape=jax.ShapeDtypeStruct((VIEWS, rows, width), f32),
            input_output_aliases={6: 0} if local else {},
        )(x, coef, prefix, steps, run, skip, *local),)
    (local,) = local
    block = lambda *dims: pl.BlockSpec((1, *dims), lambda v, i: (v, i) + (0,) * (len(dims) - 1))
    entering = pl.BlockSpec((1, STATE, width), lambda v, i: (v, 0, 0))

    span = min(rows, 512)
    mixed, squares = call(
        functools.partial(incoming_kernel, heads), "incoming",
        VIEWS * rows * STATE * width * 8, VIEWS * rows * 8192,
        grid=(VIEWS, rows // span),
        in_specs=[
            entering, entering,
            block(span, 4 * STATE), block(span, LANES), block(span, width)],
        out_specs=[block(span, width), pl.BlockSpec((1, 8, span), lambda v, i: (v, 0, i))],
        out_shape=[
            jax.ShapeDtypeStruct((VIEWS, rows, width), f32),
            jax.ShapeDtypeStruct((VIEWS, 8, rows), f32),
        ],
        scratch_shapes=[pltpu.VMEM((2, 2 * STATE, width), bf16)],
    )(forward_in, reverse_in, coef, pos, local)

    square_total = jnp.sum(lax.all_gather(squares[:, 0, :], "fsdp"), axis=0)
    scaling = lax.rsqrt(square_total / inner + 1e-05)
    normed = (mixed * scaling[:, :, None] * gain[None]).astype(bf16)
    outgoing = normed.reshape(VIEWS, shards, row_count, width).transpose(1, 0, 2, 3)
    arrived = lax.all_to_all(outgoing, "fsdp", split_axis=0, concat_axis=0)

    out_own = out_all.reshape(heads, shards, HEAD_DIM, D).transpose(1, 0, 2, 3)
    out_own = out_own.reshape(shards, width, D)
    tile = min(row_count, 128)
    grads, losses, head_term = call(
        functools.partial(tail_kernel, shards, loss_scale / total_patches), "tail",
        VIEWS * row_count * D * 3000, 6 << 20,
        grid=(row_count // tile,),
        in_specs=[
            pl.BlockSpec((shards, VIEWS, tile, width), lambda i: (0, 0, i, 0)),
            fixed(shards, width, D), fixed(D, CLASSES),
            pl.BlockSpec((tile, D), lambda i: (i, 0)),
            fixed(VIEWS, D),
            pl.BlockSpec((tile, 1), lambda i: (i, 0))],
        out_specs=[
            pl.BlockSpec((VIEWS, tile, CLASSES), lambda i: (0, i, 0)),
            pl.BlockSpec((tile, 1), lambda i: (i, 0)),
            fixed(D, CLASSES)],
        out_shape=[
            jax.ShapeDtypeStruct((VIEWS, row_count, CLASSES), bf16),
            jax.ShapeDtypeStruct((row_count, 1), f32),
            jax.ShapeDtypeStruct((D, CLASSES), f32),
        ],
    )(arrived, out_own, head_weight, patches, scales, labels[:, None])

    if ctx_count * shards == HEADS:
        grads_all = lax.all_gather(grads, "fsdp")
        grad_rows = call(
            functools.partial(grad_kernel, shards), "grads",
            VIEWS * rows * D * (width + CLASSES) * 2, 8 << 20,
            grid=(VIEWS, shards),
            in_specs=[
                pl.BlockSpec((1, row_count, width), lambda v, s: (v, s, 0)),
                pl.BlockSpec((1, 1, row_count, CLASSES), lambda v, s: (s, v, 0, 0)),
                fixed(D, CLASSES)],
            out_specs=fixed(width, D),
            out_shape=jax.ShapeDtypeStruct((width, D), f32),
        )(normed, grads_all, head_weight)
        grad_out = scatter_sum(grad_rows, "ctx", ctx_count)
    else:
        grad_hidden = lax.dot_general(
            grads, head_weight, (((2,), (1,)), ((), ())), preferred_element_type=f32
        ).astype(bf16)
        grad_rows = lax.dot_general(
            arrived, grad_hidden, (((1, 2), (0, 1)), ((), ())), preferred_element_type=f32
        )
        grad_rows = grad_rows.reshape(shards, heads, HEAD_DIM, D).transpose(1, 0, 2, 3)
        grad_out = lax.psum_scatter(
            grad_rows.reshape(inner, D), ("ctx", "fsdp"), scatter_dimension=0, tiled=True
        )
    grad_head = scatter_sum(head_term, ("ctx", "fsdp"), ctx_count * shards)
    return (grad_out, grad_head, losses[:, 0])


def solution(mesh):
    return jax.shard_map(
        on_device,
        mesh=mesh,
        in_specs=(
            P(("groups", "ctx", "fsdp"), None),
            P(("groups", "ctx", "fsdp")),
            P("groups", None),
            P("groups", None),
            P(),
            P("fsdp", None),
            P("fsdp", None),
            P(),
            P(),
            P(),
            P(),
            P("fsdp", None),
            P(),
        ),
        out_specs=(
            P(("groups", "ctx", "fsdp"), None),
            P(("groups", "ctx", "fsdp"), None),
            P(("groups", "ctx", "fsdp")),
        ),
        check_vma=False,
    )
```

```python
import functools
import jax
import jax.numpy as jnp
from jax import lax
from jax.experimental import pallas as pl
from jax.experimental.pallas import tpu as pltpu
from jax.sharding import PartitionSpec as P

D = 1024
HEADS = 16
HEAD_DIM = 64
STATE = 128
CLASSES = 128
VIEWS = 3
NOPS = 9
WIDTH_AUG = 3
BLOCK = 128
LANES = 128
LOG_ROWS = 8


loss_scale = 256.0
mix_lambda = 12.0
highest = lax.Precision.HIGHEST
f32 = jnp.float32
bf16 = jnp.bfloat16


def view_scales(op_ids, mix_codes, aug_gains):
    code_values = mix_codes.astype(jnp.float32)
    weights = code_values[:, :WIDTH_AUG] / jnp.sum(
        code_values[:, :WIDTH_AUG], axis=1, keepdims=True
    )
    keep_share = code_values[:, WIDTH_AUG] / 9.0
    onehot = (op_ids[:, :, None] == jnp.arange(NOPS, dtype=jnp.int32)[None, None, :]).astype(
        jnp.float32
    )
    op_weights = jnp.sum(onehot * weights[:, :, None], axis=1)
    mixed_gain = jnp.dot(op_weights, aug_gains, precision=highest)
    scaled = keep_share[:, None] + (1.0 - keep_share[:, None]) * mixed_gain
    return jnp.concatenate([jnp.ones((1, D), jnp.float32), scaled], axis=0)


def halves(value):
    high = value.astype(bf16)
    return high, (value - high.astype(f32)).astype(bf16)


def thirds(value):
    high = value.astype(bf16)
    rest = value - high.astype(f32)
    mid = rest.astype(bf16)
    return high, mid, (rest - mid.astype(f32)).astype(bf16)


def dot(a, b, dims=((1,), (0,))):
    return lax.dot_general(a, b, (dims, ((), ())), preferred_element_type=f32)


def spread(columns, first, heads):
    rows = columns.shape[0]
    lane = lax.broadcasted_iota(jnp.int32, (rows, LANES), 1)
    pieces = []
    for h in range(first, first + heads, 2):
        left = jnp.broadcast_to(columns[:, h : h + 1], (rows, LANES))
        right = jnp.broadcast_to(columns[:, h + 1 : h + 2], (rows, LANES))
        pieces.append(jnp.where(lane < HEAD_DIM, left, right))
    return jnp.concatenate(pieces, axis=1) if len(pieces) > 1 else pieces[0]


def project_kernel(place_ref, patches_ref, scale_ref, weight_ref, x_ref, coef_ref, raw_ref):
    width = x_ref.shape[2]
    patches = patches_ref[...].astype(f32)
    for v in range(VIEWS):
        view = (scale_ref[v : v + 1, :] * patches).astype(bf16)
        depth = weight_ref.shape[1]
        out = sum(
            dot(view[:, s * depth : (s + 1) * depth], weight_ref[s ^ place_ref[0]])
            for s in range(weight_ref.shape[0])
        )
        x_ref[v] = out[:, :width].astype(bf16)
        coef_ref[v] = out[:, width : width + 4 * STATE].astype(bf16)
        raw_ref[v] = out[:, width + 4 * STATE :]


def states_kernel(heads, raw_ref, x_ref, coef_ref, bias_ref, rate_ref,
                  final_ref, prefix_ref, steps_ref, run_ref, pos_ref):
    rows, width = x_ref.shape[1:]
    pieces = rows // BLOCK
    row = lax.broadcasted_iota(jnp.int32, (BLOCK, BLOCK), 0)
    col = lax.broadcasted_iota(jnp.int32, (BLOCK, BLOCK), 1)
    lower = (row >= col).astype(f32).astype(bf16)
    upper = (row <= col).astype(f32).astype(bf16)
    is_forward = col < heads

    def first_pass(i, carried):
        state, total = carried
        at = pl.ds(pl.multiple_of(i * BLOCK, BLOCK), BLOCK)
        raw = raw_ref[0, at, :] + bias_ref[...]
        steps = jnp.maximum(raw, 0.0) + jnp.log1p(jnp.exp(-jnp.abs(raw)))
        parts = thirds(steps * rate_ref[...])
        down = sum(dot(lower, part) for part in parts)
        up = sum(dot(upper, part) for part in parts)
        run = jnp.where(is_forward, down, up)
        steps_ref[0, at, :] = steps
        run_ref[0, at, :] = run
        pos_ref[0, at, :] = run + total
        last = jnp.where(is_forward[:1], run[BLOCK - 1 :], run[:1])
        x = x_ref[0, at, :].astype(f32)
        weight = spread(jnp.exp(last - run) * steps, 0, heads)
        high, low = halves(weight * x)
        write = coef_ref[0, at, :STATE]
        fresh = dot(write, high, ((0,), (0,))) + dot(write, low, ((0,), (0,)))
        s_high, s_low = halves(state)
        prefix_ref[0, 0, i, :STATE, :] = s_high
        prefix_ref[0, 0, i, STATE:, :] = s_low
        return spread(jnp.exp(last), 0, heads) * state + fresh, total + last

    zero = jnp.zeros((STATE, width), f32)
    no_log = jnp.zeros((1, LANES), f32)
    state, total = lax.fori_loop(0, pieces, first_pass, (zero, no_log), unroll=4)
    final_ref[0, 0, :STATE, :] = state
    final_ref[0, 0, STATE:, :] = jnp.broadcast_to(spread(total, 0, heads), (LOG_ROWS, width))

    def second_pass(k, carried):
        state, total = carried
        i = pieces - 1 - k
        at = pl.ds(pl.multiple_of(i * BLOCK, BLOCK), BLOCK)
        run = run_ref[0, at, :]
        last = run[:1]
        pos_ref[0, at, :] = jnp.where(is_forward, pos_ref[0, at, :], run + total)
        x = x_ref[0, at, :].astype(f32)
        weight = spread(jnp.exp(last - run) * steps_ref[0, at, :], heads, heads)
        high, low = halves(weight * x)
        write = coef_ref[0, at, 2 * STATE : 3 * STATE]
        fresh = dot(write, high, ((0,), (0,))) + dot(write, low, ((0,), (0,)))
        s_high, s_low = halves(state)
        prefix_ref[0, 1, i, :STATE, :] = s_high
        prefix_ref[0, 1, i, STATE:, :] = s_low
        return spread(jnp.exp(last), heads, heads) * state + fresh, total + last

    state, total = lax.fori_loop(0, pieces, second_pass, (zero, no_log), unroll=4)
    final_ref[0, 1, :STATE, :] = state
    final_ref[0, 1, STATE:, :] = jnp.broadcast_to(spread(total, heads, heads), (LOG_ROWS, width))


def inside_kernel(heads, x_ref, coef_ref, prefix_ref, steps_ref, run_ref, skip_ref, *rest):
    out_ref = rest[-1]
    row = lax.broadcasted_iota(jnp.int32, (BLOCK, BLOCK), 0)
    col = lax.broadcasted_iota(jnp.int32, (BLOCK, BLOCK), 1)
    below, above = row > col, row < col
    x = x_ref[0]
    steps_t = steps_ref[0].T
    run = run_ref[0]
    run_t = run.T
    coef = coef_ref[0]
    write_f, read_f = coef[:, :STATE], coef[:, STATE : 2 * STATE]
    write_r, read_r = coef[:, 2 * STATE : 3 * STATE], coef[:, 3 * STATE :]
    score_f = dot(read_f, write_f, ((1,), (1,)))
    score_r = dot(read_r, write_r, ((1,), (1,)))
    lane = lax.broadcasted_iota(jnp.int32, (BLOCK, LANES), 1)
    zero = jnp.zeros((BLOCK, LANES), bf16)
    pieces = []
    for pair in range(heads // 2):
        highs, lows = [], []
        for h in (2 * pair, 2 * pair + 1):
            r = heads + h
            gap = jnp.where(
                below, run[:, h : h + 1] - run_t[h : h + 1], run[:, r : r + 1] - run_t[r : r + 1]
            )
            gap = jnp.where(row == col, 0.0, gap)
            from_f = score_f * steps_t[h : h + 1]
            from_r = score_r * steps_t[r : r + 1]
            weight = jnp.where(below, from_f, jnp.where(above, from_r, from_f + from_r))
            high, low = halves(weight * jnp.exp(gap))
            highs.append(high)
            lows.append(low)
        values = x[:, pair * LANES : (pair + 1) * LANES]
        stacked = jnp.concatenate(
            [jnp.where(lane < HEAD_DIM, values, zero), jnp.where(lane < HEAD_DIM, zero, values)],
            axis=0,
        )
        pieces.append(
            dot(jnp.concatenate(highs, axis=1), stacked)
            + dot(jnp.concatenate(lows, axis=1), stacked)
        )
    inside = jnp.concatenate(pieces, axis=1) if len(pieces) > 1 else pieces[0]
    grown = jnp.exp(run)
    carried_f = dot(jnp.concatenate([read_f, read_f], axis=1), prefix_ref[0, 0, 0])
    carried_r = dot(jnp.concatenate([read_r, read_r], axis=1), prefix_ref[0, 1, 0])
    out_ref[0] = (
        inside
        + spread(grown, 0, heads) * carried_f
        + spread(grown, heads, heads) * carried_r
        + skip_ref[...] * x.astype(f32)
    )


def incoming_kernel(heads, forward_ref, reverse_ref, coef_ref, pos_ref, local_ref,
                    mixed_ref, square_ref, held):
    width = local_ref.shape[2]

    @pl.when(pl.program_id(1) == 0)
    def _():
        for way, before in enumerate((forward_ref, reverse_ref)):
            high, low = halves(before[0])
            held[way, :STATE, :] = high
            held[way, STATE:, :] = low

    grown = jnp.exp(pos_ref[0])
    coef = coef_ref[0]
    read_f = coef[:, STATE : 2 * STATE]
    read_r = coef[:, 3 * STATE :]
    mixed = (
        local_ref[0]
        + spread(grown, 0, heads) * dot(jnp.concatenate([read_f, read_f], axis=1), held[0])
        + spread(grown, heads, heads) * dot(jnp.concatenate([read_r, read_r], axis=1), held[1])
    )
    mixed_ref[0] = mixed
    ones = jnp.ones((8, width), bf16)
    square_ref[0] = sum(dot(ones, part, ((1,), (1,))) for part in thirds(mixed * mixed))


def tail_kernel(shards, factor, normed_ref, out_w_ref, head_ref, patches_ref, scale_ref,
                label_ref, logit_ref, loss_ref, head_grad_ref, hidden_ref=None):
    rows = patches_ref.shape[0]
    head = head_ref[...]
    patches = patches_ref[...].astype(f32)
    hiddens, logs = [], []
    for v in range(VIEWS):
        total = dot(normed_ref[0, v], out_w_ref[0])
        for s in range(1, shards):
            total += dot(normed_ref[s, v], out_w_ref[s])
        view = (scale_ref[v : v + 1, :] * patches).astype(bf16)
        hidden = (view.astype(f32) + total).astype(bf16)
        hiddens.append(hidden)
        logits = dot(hidden, head)
        shifted = logits - jnp.max(logits, axis=1, keepdims=True)
        logs.append(shifted - jnp.log(jnp.sum(jnp.exp(shifted), axis=1, keepdims=True)))
    top = jnp.maximum(jnp.maximum(logs[0], logs[1]), logs[2])
    mean = top + jnp.log(sum(jnp.exp(log - top) for log in logs)) - jnp.log(f32(VIEWS))
    lane = lax.broadcasted_iota(jnp.int32, (rows, CLASSES), 1)
    onehot = (lane == label_ref[...]).astype(f32)
    spread_sum = jnp.zeros((rows, 1), f32)
    grads = []
    for v in range(VIEWS):
        prob = jnp.exp(logs[v])
        gap = logs[v] - mean
        inner = jnp.sum(prob * gap, axis=1, keepdims=True)
        spread_sum += inner
        grad = (mix_lambda / VIEWS) * prob * (gap - inner)
        if v == 0:
            grad += prob - onehot
        grads.append((factor * grad).astype(bf16))
        logit_ref[v] = grads[v]
    cross = -jnp.sum(onehot * logs[0], axis=1, keepdims=True)
    loss_ref[...] = cross + mix_lambda * (spread_sum / VIEWS)
    update = sum(dot(hiddens[v], grads[v], ((0,), (0,))) for v in range(VIEWS))

    @pl.when(pl.program_id(0) == 0)
    def _():
        head_grad_ref[...] = update

    @pl.when(pl.program_id(0) > 0)
    def _():
        head_grad_ref[...] += update


def grad_kernel(shards, normed_ref, logit_ref, head_ref, out_ref):
    grads = logit_ref[0, 0]
    hidden = dot(grads, head_ref[...], ((1,), (1,))).astype(bf16)
    update = dot(normed_ref[0], hidden, ((0,), (0,)))
    first = (pl.program_id(0) == 0) & (pl.program_id(1) == 0)

    @pl.when(first)
    def _():
        out_ref[...] = update

    @pl.when(jnp.logical_not(first))
    def _():
        out_ref[...] += update


def call(kernel, name, flops, moved, limit=48 << 20, **options):
    return pl.pallas_call(
        kernel,
        name=name,
        compiler_params=pltpu.CompilerParams(vmem_limit_bytes=limit),
        cost_estimate=pl.CostEstimate(flops=flops, bytes_accessed=moved, transcendentals=0),
        **options,
    )


def carried_in(state, decay, axis, reverse):
    count = lax.axis_size(axis)
    if reverse:
        hops = [(j, j - 1) for j in range(1, count)]
    else:
        hops = [(j, j + 1) for j in range(count - 1)]
    sent, got = state, jnp.zeros_like(state)
    for hop in range(count - 1):
        got = lax.ppermute(sent, axis, hops)
        sent = decay * got + state
    return got


def scatter_sum(terms, axes, count):
    blocks = terms.reshape(count, -1, terms.shape[1])
    return jnp.sum(lax.all_to_all(blocks, axes, split_axis=0, concat_axis=0), axis=0)


def on_device(
    patches,
    labels,
    op_ids,
    mix_codes,
    aug_gains,
    in_weight,
    dt_weight,
    dt_bias,
    decay_log,
    skip_gain,
    norm_gain,
    out_weight,
    head_weight,
):
    row_count = patches.shape[0]
    ctx_count = lax.axis_size("ctx")
    shards = lax.axis_size("fsdp")
    place = lax.axis_index("fsdp")
    total_patches = row_count * ctx_count * shards
    inner = out_weight.shape[0] * shards
    heads = HEADS // shards
    width = heads * HEAD_DIM
    rows = row_count * shards
    pieces = rows // BLOCK

    if shards == 4:
        across = lax.ppermute(patches, "fsdp", [(f, f ^ 2) for f in range(shards)])
        beside = lax.ppermute(patches, "fsdp", [(f, f ^ 1) for f in range(shards)])
        corner = lax.ppermute(across, "fsdp", [(f, f ^ 1) for f in range(shards)])
        patches_all = jnp.concatenate([patches, beside, across, corner], axis=0)
        flip = place
    else:
        patches_all = lax.all_gather(patches, "fsdp", axis=0, tiled=True)
        flip = jnp.zeros_like(place)
    columns_in = inner + 4 * STATE
    depth = in_weight.shape[0]
    sent_weight = jnp.concatenate(
        [
            in_weight[:, :inner]
            .reshape(depth, heads, shards, HEAD_DIM)
            .transpose(2, 0, 1, 3)
            .reshape(shards, depth, width),
            jnp.broadcast_to(in_weight[None, :, inner:], (shards, depth, 4 * STATE)),
            dt_weight.reshape(depth, 2 * heads, shards).transpose(2, 0, 1),
            jnp.zeros((shards, depth, LANES - 2 * heads), bf16),
        ],
        axis=2,
    )
    if shards == 4:
        move = lambda part, r: lax.ppermute(part, "fsdp", [(f, f ^ r) for f in range(shards)])
        pick = lambda r: lax.dynamic_index_in_dim(sent_weight, place ^ r, 0, False)
        split = width + 4 * STATE
        far = move(pick(2), 2)
        third = pick(3)
        relayed = move(jnp.concatenate([third[:, :width], third[:, split:]], axis=1), 2)
        near = move(pick(1), 1)
        relayed = jnp.concatenate(
            [relayed[:, :width], far[:, width:split], relayed[:, width:]], axis=1
        )
        mine_weight = jnp.stack([pick(0), near, far, move(relayed, 1)])
    else:
        mine_weight = lax.all_to_all(sent_weight, "fsdp", split_axis=0, concat_axis=0)
    scales = view_scales(op_ids, mix_codes, aug_gains)
    tile = min(row_count, 128)
    per = row_count // tile
    placed = lambda s, i, flip_ref: ((s ^ flip_ref[0]) * per + i, 0)
    piece = lambda lanes: pl.BlockSpec((VIEWS, tile, lanes), lambda s, i, _: (0, s * per + i, 0))
    constant = lambda *dims: pl.BlockSpec(dims, lambda *_: (0,) * len(dims))
    x, coef, raw = call(
        project_kernel, "project",
        VIEWS * rows * D * (width + 5 * STATE) * 2, rows * D * 8,
        grid_spec=pltpu.PrefetchScalarGridSpec(
            num_scalar_prefetch=1,
            grid=(shards, per),
            in_specs=[pl.BlockSpec((tile, D), placed), constant(VIEWS, D),
                      constant(shards, depth, width + 5 * STATE)],
            out_specs=[piece(width), piece(4 * STATE), piece(LANES)],
        ),
        out_shape=[
            jax.ShapeDtypeStruct((VIEWS, rows, width), bf16),
            jax.ShapeDtypeStruct((VIEWS, rows, 4 * STATE), bf16),
            jax.ShapeDtypeStruct((VIEWS, rows, LANES), f32),
        ],
    )(flip.reshape(1).astype(jnp.int32), patches_all, scales, mine_weight)
    raw, out_later = lax.optimization_barrier((raw, out_weight))
    out_all = lax.all_gather(out_later, "fsdp", axis=0, tiled=True)

    def local_lanes(values):
        picked = lax.dynamic_index_in_dim(values.reshape(2 * heads, shards), place, 1, False)
        return jnp.pad(picked, (0, LANES - 2 * heads))[None, :]

    bias = local_lanes(dt_bias)
    rate = local_lanes(-jnp.exp(decay_log))
    skip = lax.dynamic_index_in_dim(skip_gain.reshape(heads, shards), place, 1, False)
    skip = jnp.repeat(skip, HEAD_DIM)[None, :]
    gain = norm_gain.reshape(heads, shards, HEAD_DIM)
    gain = lax.dynamic_index_in_dim(gain, place, 1, False).reshape(1, width)

    whole = lambda *dims: pl.BlockSpec((1, *dims), lambda v: (v,) + (0,) * len(dims))
    fixed = lambda *dims: pl.BlockSpec(dims, lambda *_: (0,) * len(dims))
    final, prefix, steps, run, pos = call(
        functools.partial(states_kernel, heads), "states",
        VIEWS * rows * STATE * width * 8, VIEWS * rows * 8192,
        grid=(VIEWS,),
        in_specs=[whole(rows, LANES), whole(rows, width), whole(rows, 4 * STATE),
                  fixed(1, LANES), fixed(1, LANES)],
        out_specs=[whole(2, STATE + LOG_ROWS, width), whole(2, pieces, 2 * STATE, width),
                   whole(rows, LANES), whole(rows, LANES), whole(rows, LANES)],
        out_shape=[
            jax.ShapeDtypeStruct((VIEWS, 2, STATE + LOG_ROWS, width), f32),
            jax.ShapeDtypeStruct((VIEWS, 2, pieces, 2 * STATE, width), bf16),
            jax.ShapeDtypeStruct((VIEWS, rows, LANES), f32),
            jax.ShapeDtypeStruct((VIEWS, rows, LANES), f32),
            jax.ShapeDtypeStruct((VIEWS, rows, LANES), f32),
        ],
    )(raw, x, coef, bias, rate)
    decay = jnp.exp(final[:, :, STATE : STATE + 1, :])
    forward_in = carried_in(final[:, 0, :STATE], decay[:, 0], "ctx", False)
    reverse_in = carried_in(final[:, 1, :STATE], decay[:, 1], "ctx", True)

    local = ()
    for v in range(VIEWS):
        at = lambda *dims, v=v: pl.BlockSpec(
            (1, *dims), lambda i: (v, i) + (0,) * (len(dims) - 1)
        )
        local = (call(
            functools.partial(inside_kernel, heads), "inside",
            rows * D * 8192, rows * 8192,
            grid=(pieces,),
            in_specs=[at(BLOCK, width), at(BLOCK, 4 * STATE),
                      pl.BlockSpec((1, 2, 1, 2 * STATE, width), lambda i, v=v: (v, 0, i, 0, 0)),
                      at(BLOCK, LANES), at(BLOCK, LANES), fixed(1, width)]
            + [pl.BlockSpec(memory_space=pl.ANY)] * len(local),
            out_specs=at(BLOCK, width),
            out_shape=jax.ShapeDtypeStruct((VIEWS, rows, width), f32),
            input_output_aliases={6: 0} if local else {},
        )(x, coef, prefix, steps, run, skip, *local),)
    (local,) = local
    block = lambda *dims: pl.BlockSpec((1, *dims), lambda v, i: (v, i) + (0,) * (len(dims) - 1))
    entering = pl.BlockSpec((1, STATE, width), lambda v, i: (v, 0, 0))

    span = min(rows, 512)
    mixed, squares = call(
        functools.partial(incoming_kernel, heads), "incoming",
        VIEWS * rows * STATE * width * 8, VIEWS * rows * 8192,
        grid=(VIEWS, rows // span),
        in_specs=[
            entering, entering,
            block(span, 4 * STATE), block(span, LANES), block(span, width)],
        out_specs=[block(span, width), pl.BlockSpec((1, 8, span), lambda v, i: (v, 0, i))],
        out_shape=[
            jax.ShapeDtypeStruct((VIEWS, rows, width), f32),
            jax.ShapeDtypeStruct((VIEWS, 8, rows), f32),
        ],
        scratch_shapes=[pltpu.VMEM((2, 2 * STATE, width), bf16)],
    )(forward_in, reverse_in, coef, pos, local)

    square_total = jnp.sum(lax.all_gather(squares[:, 0, :], "fsdp"), axis=0)
    scaling = lax.rsqrt(square_total / inner + 1e-05)
    normed = (mixed * scaling[:, :, None] * gain[None]).astype(bf16)
    outgoing = normed.reshape(VIEWS, shards, row_count, width).transpose(1, 0, 2, 3)
    arrived = lax.all_to_all(outgoing, "fsdp", split_axis=0, concat_axis=0)

    out_own = out_all.reshape(heads, shards, HEAD_DIM, D).transpose(1, 0, 2, 3)
    out_own = out_own.reshape(shards, width, D)
    tile = min(row_count, 128)
    grads, losses, head_term = call(
        functools.partial(tail_kernel, shards, loss_scale / total_patches), "tail",
        VIEWS * row_count * D * 3000, 6 << 20,
        grid=(row_count // tile,),
        in_specs=[
            pl.BlockSpec((shards, VIEWS, tile, width), lambda i: (0, 0, i, 0)),
            fixed(shards, width, D), fixed(D, CLASSES),
            pl.BlockSpec((tile, D), lambda i: (i, 0)),
            fixed(VIEWS, D),
            pl.BlockSpec((tile, 1), lambda i: (i, 0))],
        out_specs=[
            pl.BlockSpec((VIEWS, tile, CLASSES), lambda i: (0, i, 0)),
            pl.BlockSpec((tile, 1), lambda i: (i, 0)),
            fixed(D, CLASSES)],
        out_shape=[
            jax.ShapeDtypeStruct((VIEWS, row_count, CLASSES), bf16),
            jax.ShapeDtypeStruct((row_count, 1), f32),
            jax.ShapeDtypeStruct((D, CLASSES), f32),
        ],
    )(arrived, out_own, head_weight, patches, scales, labels[:, None])

    if ctx_count * shards == HEADS:
        grads_all = lax.all_gather(grads, "fsdp")
        grad_rows = call(
            functools.partial(grad_kernel, shards), "grads",
            VIEWS * rows * D * (width + CLASSES) * 2, 8 << 20,
            grid=(VIEWS, shards),
            in_specs=[
                pl.BlockSpec((1, row_count, width), lambda v, s: (v, s, 0)),
                pl.BlockSpec((1, 1, row_count, CLASSES), lambda v, s: (s, v, 0, 0)),
                fixed(D, CLASSES)],
            out_specs=fixed(width, D),
            out_shape=jax.ShapeDtypeStruct((width, D), f32),
        )(normed, grads_all, head_weight)
        grad_out = scatter_sum(grad_rows, "ctx", ctx_count)
    else:
        grad_hidden = lax.dot_general(
            grads, head_weight, (((2,), (1,)), ((), ())), preferred_element_type=f32
        ).astype(bf16)
        grad_rows = lax.dot_general(
            arrived, grad_hidden, (((1, 2), (0, 1)), ((), ())), preferred_element_type=f32
        )
        grad_rows = grad_rows.reshape(shards, heads, HEAD_DIM, D).transpose(1, 0, 2, 3)
        grad_out = lax.psum_scatter(
            grad_rows.reshape(inner, D), ("ctx", "fsdp"), scatter_dimension=0, tiled=True
        )
    grad_head = scatter_sum(head_term, ("ctx", "fsdp"), ctx_count * shards)
    return (grad_out, grad_head, losses[:, 0])


def solution(mesh):
    return jax.shard_map(
        on_device,
        mesh=mesh,
        in_specs=(
            P(("groups", "ctx", "fsdp"), None),
            P(("groups", "ctx", "fsdp")),
            P("groups", None),
            P("groups", None),
            P(),
            P("fsdp", None),
            P("fsdp", None),
            P(),
            P(),
            P(),
            P(),
            P("fsdp", None),
            P(),
        ),
        out_specs=(
            P(("groups", "ctx", "fsdp"), None),
            P(("groups", "ctx", "fsdp"), None),
            P(("groups", "ctx", "fsdp")),
        ),
        check_vma=False,
    )
```
